256 devices in a mesh: row: 16 (over y_hi, z), col: 16 (over y_lo, x, core).
Axes of the slice: x: 4, y: 4 (y_hi: 2, y_lo: 2; y = y_hi * 2 + y_lo), z: 8, core: 2. Of those that a mesh axis runs over, the one named last changes fastest.
Arguments:
- brick_velocity_stress: float32 [1024, 9, 16, 256], P(('row', 'col')), may hold values from -6 to 6
- brick_relaxation_memory: float32 [1024, 18, 16, 256], P(('row', 'col')), may hold values from -2 to 2
- brick_cell_material: int32 [1024, 16, 256], P(('row', 'col')), may hold values from 0 to 7
- brick_live: int32 [1024], P(('row', 'col')), may hold values from 0 to 1, as said below
- water_state: float32 [4, 512, 512, 128], P(None, 'row', 'col'), may hold values from -6 to 6
- water_material: int32 [512, 512, 128], P('row', 'col'), may hold values from 0 to 7
- material_table: float32 [8, 8], replicated, may hold values from 0.01 to 0.95, as said below
Outputs:
- motion_out: float32 [1024, 9, 16, 256], P(('row', 'col'))
- memory_out: float32 [1024, 18, 16, 256], P(('row', 'col'))
- water_out: float32 [4, 512, 512, 128], P(None, 'row', 'col')
The draws below stay inside these ranges and needn't reach their ends.
Inputs may be any that keep to these rules, and one draw needn't show every extreme that they name: `brick_live`: tiles j and j + 8 of one row of tiles hold 4 live bricks together; in every row some tile holds 4 or none. `material_table`: column 0 is the buoyancy, 1 the first Lame constant (the bulk modulus of water cells), 2 the shear modulus, 3 to 5 the retentions of the three mechanisms, 6 and 7 the anelastic Lame constant and shear modulus.
All inputs are finite; a program needn't handle non-finite values.
Results may differ from the reference program's by a relative error of at most 0.00011.
Values sent between devices are 32-bit elements; how exact they have to be, the bound alone decides.
A program may use at most 128 MiB of HBM per device.

```python
import jax
import jax.numpy as jnp
from jax import lax

BRICK_EDGE_CELLS = 16
NZ = 128
STEPS = 3
MATERIAL_COUNT = 8
TILE_COUNT_X = 16
TILE_COUNT_Y = 16
NX = 512
NY = 512
BRICK_SLOT_COUNT = 1024
BRICK_FACE_CELLS = 256


def draw_brick_live(key, part):
    keys = jax.random.split(jax.random.fold_in(key, 17), 4)
    half_count = TILE_COUNT_Y // 2
    lower = jax.random.randint(keys[0], (TILE_COUNT_X, half_count), 0, 5)
    chosen = jax.random.randint(keys[1], (TILE_COUNT_X,), 0, half_count)
    extreme = jax.random.randint(keys[2], (TILE_COUNT_X,), 0, 2) * 4
    places = jnp.arange(half_count, dtype=jnp.int32)
    lower = jnp.where(places[None, :] == chosen[:, None], extreme[:, None], lower)
    counts = jnp.concatenate([lower, 4 - lower], axis=1)
    scores = jax.random.randint(keys[3], (TILE_COUNT_X, TILE_COUNT_Y, 4), 0, 1 << 20) * 4 + jnp.arange(4, dtype=jnp.int32)
    ranks = jnp.argsort(jnp.argsort(scores, axis=-1), axis=-1)
    alive = (ranks < counts[..., None]).astype(jnp.int32)
    return alive.reshape((-1,))


def draw_material_table(key, part):
    lower = jnp.array([0.4, 0.05, 0.02, 0.3, 0.5, 0.7, 0.01, 0.01], jnp.float32)
    upper = jnp.array([0.8, 0.15, 0.08, 0.6, 0.8, 0.95, 0.05, 0.03], jnp.float32)
    spread = jax.random.uniform(jax.random.fold_in(key, 29), (MATERIAL_COUNT, 8), jnp.float32)
    return lower[None, :] + (upper - lower)[None, :] * spread


def plant(result, own_key, least, top_value):
    longest = result.shape.index(max(result.shape))
    spots = []
    for shift in (0, 1):
        where = [jax.random.randint(jax.random.fold_in(own_key, axis), (), 0, length) for axis, length in enumerate(result.shape)]
        where[longest] = (where[longest] + shift) % result.shape[longest]
        spots.append(tuple(where))
    return result.at[spots[0]].set(least).at[spots[1]].set(top_value)


def shard_levels(key, dims, cuts, low, largest):
    gain, own = 1.0, jax.random.fold_in(key, 6)
    for position, shards_of in cuts:
        steps = jnp.exp(jax.random.uniform(jax.random.fold_in(own, position), (shards_of,), jnp.float32, low / len(cuts), largest / len(cuts)))
        gain = gain * jnp.repeat(steps, dims[position] // shards_of).reshape([-1 if axis == position else 1 for axis in range(len(dims))])
    return gain


def normal_values(own_key, shape, deviation, bound, shards=(), kind=jnp.bfloat16):
    loudness = shard_levels(own_key, shape, shards, -0.22, 0.18) if shards else 1.0
    drawn = jax.random.normal(own_key, shape, jnp.float32) * deviation * loudness
    return jnp.minimum(jnp.maximum(drawn, -bound), bound).astype(kind)


def setup_inputs(seed: int = 0) -> dict:
    seeds = jax.random.split(jax.random.key(seed), 8)
    brick_velocity_stress = normal_values(seeds[0], (BRICK_SLOT_COUNT, 9, BRICK_EDGE_CELLS, BRICK_FACE_CELLS), 1.0, 6.0, ((0, 256),), jnp.float32)
    brick_relaxation_memory = normal_values(seeds[1], (BRICK_SLOT_COUNT, 18, BRICK_EDGE_CELLS, BRICK_FACE_CELLS), 0.3, 2.0, ((0, 256),), jnp.float32)
    brick_cell_material = plant(jax.random.randint(seeds[2], (BRICK_SLOT_COUNT, BRICK_EDGE_CELLS, BRICK_FACE_CELLS), 0, MATERIAL_COUNT), jax.random.fold_in(seeds[2], 1), 0, MATERIAL_COUNT - 1).astype(jnp.int32)
    brick_live = draw_brick_live(jax.random.fold_in(seeds[7], 71), 0)
    water_state = normal_values(seeds[4], (4, NX, NY, NZ), 1.0, 6.0, ((1, 16), (2, 16)), jnp.float32)
    water_material = plant(jax.random.randint(seeds[5], (NX, NY, NZ), 0, MATERIAL_COUNT), jax.random.fold_in(seeds[5], 1), 0, MATERIAL_COUNT - 1).astype(jnp.int32)
    material_table = draw_material_table(jax.random.fold_in(seeds[7], 71), 0)
    return {"brick_velocity_stress": brick_velocity_stress, "brick_relaxation_memory": brick_relaxation_memory, "brick_cell_material": brick_cell_material, "brick_live": brick_live, "water_state": water_state, "water_material": water_material, "material_table": material_table}


def lookup(indices, values_table, first, stop):
    levels = jnp.arange(values_table.shape[0], dtype=jnp.int32)
    onehot = (indices[None] == levels.reshape((-1,) + (1,) * indices.ndim)).astype(jnp.float32)
    return jnp.einsum('mk,m...->k...', values_table[:, first:stop], onehot, precision=lax.Precision.HIGHEST)


def along_x(field, before, beyond):
    forward = jnp.concatenate([field[..., 1:, :], beyond[..., None, :]], axis=-2)
    backward = jnp.concatenate([before[..., None, :], field[..., :-1, :]], axis=-2)
    return 0.5 * (forward - backward)


def along_y(field, before, beyond):
    extent = before.shape[-1]
    padded = jnp.concatenate([before, field, beyond], axis=-1)
    return 0.5 * (padded[..., 2 * extent:] - padded[..., :-2 * extent])


def along_z(field, before, beyond):
    extent = before.shape[-1]
    depth_pos = lax.broadcasted_iota(jnp.int32, field.shape, field.ndim - 1) % extent
    nothing = jnp.zeros_like(field[..., :1])
    forward = jnp.where(depth_pos == extent - 1, jnp.repeat(beyond, extent, axis=-1), jnp.concatenate([field[..., 1:], nothing], axis=-1))
    backward = jnp.where(depth_pos == 0, jnp.repeat(before, extent, axis=-1), jnp.concatenate([nothing, field[..., :-1]], axis=-1))
    return 0.5 * (forward - backward)


def face_layers(fields):
    extent = fields.shape[2]
    first_y = fields[..., :extent].reshape(fields.shape[:2] + (-1,))
    last_y = fields[..., -extent:].reshape(fields.shape[:2] + (-1,))
    return jnp.stack([fields[:, :, 0], fields[:, :, -1], first_y, last_y], axis=1)


def top_layer(fields):
    extent = fields.shape[2]
    return fields[..., extent - 1::extent].reshape(fields.shape[:2] + (-1,))


def brick_velocity(motion, params, nearby_cells, top_p):
    stress = motion[:, 3:9]
    extent = motion.shape[2]
    leading_axes = (motion.shape[0], extent, extent)
    blank = jnp.zeros(leading_axes, jnp.float32)

    def diff_x(comp):
        return along_x(stress[:, comp], nearby_cells[:, 0, comp], nearby_cells[:, 1, comp])

    def diff_y(comp):
        return along_y(stress[:, comp], nearby_cells[:, 2, comp].reshape(leading_axes), nearby_cells[:, 3, comp].reshape(leading_axes))

    def diff_z(comp, beyond):
        return along_z(stress[:, comp], blank, beyond)

    upper_stress = -top_p.reshape(leading_axes)
    forcing = jnp.stack([diff_x(0) + diff_y(3) + diff_z(4, blank), diff_x(3) + diff_y(1) + diff_z(5, blank), diff_x(4) + diff_y(5) + diff_z(2, upper_stress)], axis=1)
    velocity = motion[:, 0:3] + params[:, 0:1] * forcing
    return jnp.concatenate([velocity, stress], axis=1)


def brick_stress(motion, memory, params, nearby_cells, top_u):
    velocity = motion[:, 0:3]
    extent = motion.shape[2]
    leading_axes = (motion.shape[0], extent, extent)
    blank = jnp.zeros(leading_axes, jnp.float32)

    def diff_x(comp):
        return along_x(velocity[:, comp], nearby_cells[:, 0, comp], nearby_cells[:, 1, comp])

    def diff_y(comp):
        return along_y(velocity[:, comp], nearby_cells[:, 2, comp].reshape(leading_axes), nearby_cells[:, 3, comp].reshape(leading_axes))

    def diff_z(comp):
        return along_z(velocity[:, comp], blank, top_u[:, comp].reshape(leading_axes))

    strain = [diff_x(0), diff_y(1), diff_z(2), 0.5 * (diff_y(0) + diff_x(1)), 0.5 * (diff_z(0) + diff_x(2)), 0.5 * (diff_z(1) + diff_y(2))]
    dilation = strain[0] + strain[1] + strain[2]
    lame_first, shear_mod = params[:, 1], params[:, 2]
    spring_lame, spring_shear = params[:, 6], params[:, 7]
    memories = {}
    stresses = []
    for comp in range(6):
        elastic = 2.0 * shear_mod * strain[comp]
        relaxed = 2.0 * spring_shear * strain[comp]
        if comp < 3:
            elastic = elastic + lame_first * dilation
            relaxed = relaxed + spring_lame * dilation
        summed = jnp.zeros(leading_axes[:1] + (extent, extent * extent), jnp.float32)
        for mechanism in range(3):
            retain = params[:, 3 + mechanism]
            updated = retain * memory[:, 6 * mechanism + comp] + (1.0 - retain) * relaxed
            memories[6 * mechanism + comp] = updated
            summed = summed + updated
        stresses.append(motion[:, 3 + comp] + elastic - summed)
    new_memory = jnp.stack([memories[place] for place in range(18)], axis=1)
    return jnp.concatenate([velocity, jnp.stack(stresses, axis=1)], axis=1), new_memory


def vertical(field, bottom):
    nothing = jnp.zeros_like(field[..., :1])
    forward = jnp.concatenate([field[..., 1:], nothing], axis=-1)
    backward = jnp.concatenate([bottom[..., None], field[..., :-1]], axis=-1)
    return 0.5 * (forward - backward)


def water_velocity(water, buoyancy, p_padded, bottom_p):
    grad_x = 0.5 * (p_padded[2:, 1:-1] - p_padded[:-2, 1:-1])
    grad_y = 0.5 * (p_padded[1:-1, 2:] - p_padded[1:-1, :-2])
    grad_z = vertical(water[0], bottom_p)
    velocity = water[1:4] - buoyancy[None] * jnp.stack([grad_x, grad_y, grad_z])
    return jnp.concatenate([water[0:1], velocity], axis=0)


def water_pressure(water, bulk_modulus, ux_padded, uy_padded, bottom_u):
    divergence = 0.5 * (ux_padded[2:, 1:-1] - ux_padded[:-2, 1:-1]) + 0.5 * (uy_padded[1:-1, 2:] - uy_padded[1:-1, :-2]) + vertical(water[3], bottom_u)
    pressure = water[0] - bulk_modulus * divergence
    return jnp.concatenate([pressure[None], water[1:4]], axis=0)


def surface_to_slots(surface):
    leading_axes = surface.shape[:-2]
    count_lead = len(leading_axes)
    reshaped_array = surface.reshape(leading_axes + (TILE_COUNT_X, 2, BRICK_EDGE_CELLS, TILE_COUNT_Y, 2, BRICK_EDGE_CELLS))
    axis_permutation = tuple(range(count_lead)) + tuple(count_lead + place for place in (0, 3, 1, 4, 2, 5))
    return reshaped_array.transpose(axis_permutation).reshape(leading_axes + (BRICK_SLOT_COUNT, BRICK_EDGE_CELLS * BRICK_EDGE_CELLS))


def slots_to_surface(slots):
    reshaped_array = slots.reshape((TILE_COUNT_X, TILE_COUNT_Y, 2, 2, BRICK_EDGE_CELLS, BRICK_EDGE_CELLS))
    return reshaped_array.transpose((0, 2, 4, 1, 3, 5)).reshape((NX, NY))


def neighbours(side_faces):
    trailing_axes = side_faces.shape[1:]
    patch_grid = side_faces.reshape((TILE_COUNT_X, TILE_COUNT_Y, 2, 2) + trailing_axes).transpose((0, 2, 1, 3, 4, 5, 6)).reshape((2 * TILE_COUNT_X, 2 * TILE_COUNT_Y) + trailing_axes)
    padded = jnp.pad(patch_grid, ((1, 1), (1, 1), (0, 0), (0, 0), (0, 0)))
    nearby_cells = jnp.stack([padded[:-2, 1:-1, 1], padded[2:, 1:-1, 0], padded[1:-1, :-2, 3], padded[1:-1, 2:, 2]], axis=2)
    return nearby_cells.reshape((TILE_COUNT_X, 2, TILE_COUNT_Y, 2) + trailing_axes).transpose((0, 2, 1, 3, 4, 5, 6)).reshape((BRICK_SLOT_COUNT,) + trailing_axes)


def pad_plane(field):
    return jnp.pad(field, ((1, 1), (1, 1), (0, 0)))


def reference(brick_velocity_stress, brick_relaxation_memory, brick_cell_material, brick_live, water_state, water_material, material_table):
    alive_mask = brick_live.astype(jnp.float32)[:, None, None, None]
    motion = brick_velocity_stress * alive_mask
    memory = brick_relaxation_memory * alive_mask
    params = jnp.moveaxis(lookup(brick_cell_material, material_table, 0, 8), 0, 1)
    coefficients = lookup(water_material, material_table, 0, 2)
    buoyancy, bulk_modulus = coefficients[0], coefficients[1]
    water = water_state
    for instant in range(STEPS):
        nearby_cells = neighbours(face_layers(motion[:, 3:9]))
        upper_face = top_layer(motion[:, 5:6])
        bottom_p = -slots_to_surface(upper_face[:, 0])
        p_slots = surface_to_slots(water[0, :, :, 0])
        water = water_velocity(water, buoyancy, pad_plane(water[0]), bottom_p)
        motion = brick_velocity(motion, params, nearby_cells, p_slots) * alive_mask
        nearby_cells = neighbours(face_layers(motion[:, 0:3]))
        upper_face = top_layer(motion[:, 0:3])
        bottom_u = slots_to_surface(upper_face[:, 2])
        u_slots = jnp.moveaxis(surface_to_slots(water[1:4, :, :, 0]), 0, 1)
        water = water_pressure(water, bulk_modulus, pad_plane(water[1]), pad_plane(water[2]), bottom_u)
        motion, memory = brick_stress(motion, memory, params, nearby_cells, u_slots)
        motion = motion * alive_mask
        memory = memory * alive_mask
    return motion, memory, water
```

```python
import jax
import jax.numpy as jnp
from jax import lax
from jax.experimental import pallas as pl
from jax.experimental.pallas import tpu as pltpu
from jax.sharding import PartitionSpec as P

STEPS = 3
SIDE = 32
EDGE = 16
PLANES = 36
ROWS = 40
LANES = 640
INNER = 512
MESH = pl.DeviceIdType.MESH
F32 = jnp.float32


def lane_pos(shape):
    return lax.broadcasted_iota(jnp.int32, shape, len(shape) - 1)


def row_pos(shape):
    return lax.broadcasted_iota(jnp.int32, shape, len(shape) - 2)


def shift(value, amount, axis):
    amount = amount % value.shape[axis]
    return value if amount == 0 else pltpu.roll(value, amount, axis)


def pick(indices, table, column):
    bits = [(indices & (1 << bit)) != 0 for bit in range(3)]
    values = [table[level, column] for level in range(8)]
    values = [jnp.where(bits[0], values[2 * i + 1], values[2 * i]) for i in range(4)]
    values = [jnp.where(bits[1], values[2 * i + 1], values[2 * i]) for i in range(2)]
    return jnp.where(bits[2], values[1], values[0])


def strip(i):
    return pl.ds(pl.multiple_of(8 * i, 8), 8)


def kernel(
    mvs_in, mem_in, mat_in, live_in, water_in, wmat_in, table,
    motion_out, memory_out, water_out,
    B, G, CF, M, MAT, W, WM,
    tbx, tby, tbc, twx, twy, sbx, sby, swx, swy,
    rbx, rby, rbc, rwx, rwy, ebx, eby, ewx, ewy,
    load_sem, send_sem, recv_sem, xsend_sem, xrecv_sem,
):
    row, col = lax.axis_index("row"), lax.axis_index("col")
    nrow, ncol = lax.axis_size("row"), lax.axis_size("col")
    row_to = (row < nrow - 1, row > 0)
    row_from = (row > 0, row < nrow - 1)
    col_to = (col < ncol - 1, col > 0)
    col_from = (col > 0, col < ncol - 1)
    step_of = (1, -1)
    flat = W.reshape(6 * PLANES * ROWS, 128)

    def line(field, y):
        return pl.ds(field * PLANES * ROWS + y, SIDE, stride=ROWS)

    loads = [
        pltpu.make_async_copy(
            water_in, W.at[pl.ds(0, 4), pl.ds(0, SIDE), pl.ds(0, SIDE)], load_sem.at[0]
        ),
        pltpu.make_async_copy(wmat_in, WM, load_sem.at[1]),
    ]
    for s in range(4):
        rows, lanes = pl.ds(EDGE * (s // 2), EDGE), pl.ds(256 * (s % 2), 256)
        loads.append(
            pltpu.make_async_copy(mat_in.at[s], MAT.at[rows, lanes], load_sem.at[2 + s])
        )
        loads.append(
            pltpu.make_async_copy(
                mvs_in.at[s], B.at[pl.ds(0, 9), rows, lanes], load_sem.at[6 + s]
            )
        )
        loads.append(
            pltpu.make_async_copy(mem_in.at[s], M.at[:, rows, lanes], load_sem.at[10 + s])
        )
    for load in loads:
        load.start()

    barrier = pltpu.get_barrier_semaphore()
    partners = []
    for dr in (-1, 0, 1):
        for dc in (-1, 0, 1):
            if dr or dc:
                there = jnp.logical_and(
                    jnp.logical_and(row + dr >= 0, row + dr < nrow),
                    jnp.logical_and(col + dc >= 0, col + dc < ncol),
                )
                partners.append(there)

                @pl.when(there)
                def _():
                    pl.semaphore_signal(
                        barrier, inc=1, device_id=(row + dr, col + dc), device_id_type=MESH
                    )

    for t in range(2):

        @pl.when(jnp.logical_not(row_from[t]))
        def _():
            rbx[:, t] = jnp.zeros((STEPS, EDGE, INNER), F32)
            rwx[:, t] = jnp.zeros((STEPS, 2, SIDE, 128), F32)
            ebx[t] = jnp.zeros((8, INNER), F32)
            ewx[t] = jnp.zeros((2, SIDE, 128), F32)

        @pl.when(jnp.logical_not(col_from[t]))
        def _():
            rby[:, t] = jnp.zeros((STEPS, SIDE, 256), F32)
            rwy[:, t] = jnp.zeros((STEPS, 2, SIDE, 128), F32)
            eby[t] = jnp.zeros((SIDE, 128), F32)
            ewy[t] = jnp.zeros((2, SIDE, 128), F32)

        for u in range(2):

            @pl.when(jnp.logical_not(jnp.logical_and(row_from[t], col_from[u])))
            def _():
                rbc[:, 2 * t + u] = jnp.zeros((STEPS, 8, 128), F32)

    def remote(src, dst, send, recv, dr, dc):
        return pltpu.make_async_remote_copy(
            src_ref=src, dst_ref=dst, send_sem=send, recv_sem=recv,
            device_id=(row + dr, col + dc), device_id_type=MESH,
        )

    def brick_copies(n):
        out = []
        for t in range(2):
            d = step_of[t]
            out.append((
                remote(tbx.at[n, t], rbx.at[n, t], send_sem.at[n, t], recv_sem.at[n, t], d, 0),
                row_to[t], row_from[t],
            ))
            out.append((
                remote(tby.at[n, t], rby.at[n, t], send_sem.at[n, 2 + t],
                       recv_sem.at[n, 2 + t], 0, d),
                col_to[t], col_from[t],
            ))
            for u in range(2):
                q = 2 * t + u
                out.append((
                    remote(tbc.at[n, q], rbc.at[n, q], send_sem.at[n, 4 + q],
                           recv_sem.at[n, 4 + q], d, step_of[u]),
                    jnp.logical_and(row_to[t], col_to[u]),
                    jnp.logical_and(row_from[t], col_from[u]),
                ))
        return out

    def water_copies(n):
        out = []
        for t in range(2):
            d = step_of[t]
            out.append((
                remote(twx.at[n, t], rwx.at[n, t], send_sem.at[n, 8 + t],
                       recv_sem.at[n, 8 + t], d, 0),
                row_to[t], row_from[t],
            ))
            out.append((
                remote(twy.at[n, t], rwy.at[n, t], send_sem.at[n, 10 + t],
                       recv_sem.at[n, 10 + t], 0, d),
                col_to[t], col_from[t],
            ))
        return out

    def first_water_copies():
        out = []
        for t in range(2):
            d = step_of[t]
            out.append((
                remote(swx.at[t], ewx.at[t], xsend_sem.at[t], xrecv_sem.at[t], d, 0),
                row_to[t], row_from[t],
            ))
            out.append((
                remote(swy.at[t], ewy.at[t], xsend_sem.at[2 + t], xrecv_sem.at[2 + t], 0, d),
                col_to[t], col_from[t],
            ))
        return out

    def first_brick_copies():
        out = []
        for t in range(2):
            d = step_of[t]
            out.append((
                remote(sbx.at[t], ebx.at[t], xsend_sem.at[4 + t], xrecv_sem.at[4 + t], d, 0),
                row_to[t], row_from[t],
            ))
            out.append((
                remote(sby.at[t], eby.at[t], xsend_sem.at[6 + t], xrecv_sem.at[6 + t], 0, d),
                col_to[t], col_from[t],
            ))
        return out

    def start(copies):
        for copy, to, _ in copies:

            @pl.when(to)
            def _():
                copy.start()

    def arrive(copies):
        for copy, _, came in copies:

            @pl.when(came)
            def _():
                copy.wait_recv()

    def sent(copies):
        for copy, to, _ in copies:

            @pl.when(to)
            def _():
                copy.wait_send()

    pair = row_pos((8, INNER))
    tile_lane = lane_pos((SIDE, 128))

    def pack_brick(n):
        for half in range(2):
            down, up = jnp.zeros((8, INNER), F32), jnp.zeros((8, INNER), F32)
            ahead, back = jnp.zeros((SIDE, 128), F32), jnp.zeros((SIDE, 128), F32)
            for j in range(4):
                k = 4 * half + j
                if k == 7:
                    continue
                here = pair // 2 == j
                up = jnp.where(here, shift(B[3 + k, 24:32, 0:INNER], 2 * j - 6, 0), up)
                down = jnp.where(here, shift(B[3 + k, 0:8, 0:INNER], 2 * j, 0), down)
                here = tile_lane // 32 == j
                ahead = jnp.where(
                    here, shift(B[3 + k, 0:SIDE, 384:512], 32 * j - 96, 1), ahead
                )
                back = jnp.where(here, shift(B[3 + k, 0:SIDE, 0:128], 32 * j, 1), back)
            tbx[n, 0, 8 * half:8 * half + 8, :] = up
            tbx[n, 1, 8 * half:8 * half + 8, :] = down
            tby[n, 0, :, 128 * half:128 * half + 128] = ahead
            tby[n, 1, :, 128 * half:128 * half + 128] = back
        lane = lane_pos((8, 128))
        for t in range(2):
            rows = slice(24, 32) if t == 0 else slice(0, 8)
            for u in range(2):
                corner = jnp.zeros((8, 128), F32)
                for k in range(6):
                    tile = B[3 + k, rows, 384:512] if u == 0 else B[3 + k, rows, 0:128]
                    tile = shift(tile, 16 * k - (112 if u == 0 else 0), 1)
                    corner = jnp.where(lane // 16 == k, tile, corner)
                tbc[n, 2 * t + u] = corner

    def unpack_brick(n):
        for k in range(7):
            tile, j = k // 4, k % 4
            rows = slice(8 * tile, 8 * tile + 8)
            before = shift(rbx[n, 0, rows, :], 6 - 2 * j, 0)
            after = shift(rbx[n, 1, rows, :], -2 * j, 0)
            B[3 + k, 32:40, 0:INNER] = jnp.where(pair < 4, after, before)
            lanes = slice(128 * tile, 128 * tile + 128)
            before = shift(rby[n, 0, :, lanes], 96 - 32 * j, 1)
            after = shift(rby[n, 1, :, lanes], -32 * j, 1)
            B[3 + k, 0:SIDE, INNER:LANES] = jnp.where(tile_lane < 64, after, before)
        lane, sub = lane_pos((8, 128)), row_pos((8, 128))
        for k in range(6):
            top = jnp.where(
                lane < 64, shift(rbc[n, 3], -16 * k, 1), shift(rbc[n, 2], 112 - 16 * k, 1)
            )
            bottom = jnp.where(
                lane < 64, shift(rbc[n, 1], -16 * k, 1), shift(rbc[n, 0], 112 - 16 * k, 1)
            )
            B[3 + k, 32:40, INNER:LANES] = jnp.where(sub < 4, top, bottom)

    x_extra = ((B, 0), (B, 1), (B, 2), (G, 3), (G, 0), (G, 4))
    y_extra = ((B, 0), (B, 1), (B, 2), (G, 3), (G, 1), (G, 4))

    def pack_first_brick():
        down, up = jnp.zeros((8, INNER), F32), jnp.zeros((8, INNER), F32)
        ahead, back = jnp.zeros((SIDE, 128), F32), jnp.zeros((SIDE, 128), F32)
        for j in range(6):
            ref, f = x_extra[j]
            up = jnp.where(pair == j, shift(ref[f, 24:32, 0:INNER], j - 7, 0), up)
            down = jnp.where(pair == j, shift(ref[f, 0:8, 0:INNER], j, 0), down)
            ref, f = y_extra[j]
            here = tile_lane // 16 == j
            ahead = jnp.where(here, shift(ref[f, 0:SIDE, 384:512], 16 * j - 112, 1), ahead)
            back = jnp.where(here, shift(ref[f, 0:SIDE, 0:128], 16 * j, 1), back)
        sbx[0], sbx[1], sby[0], sby[1] = up, down, ahead, back

    def unpack_first_brick():
        for j in range(6):
            ref, f = x_extra[j]
            ref[f, 32:40, 0:INNER] = jnp.where(
                pair < 4, shift(ebx[1], -j, 0), shift(ebx[0], 7 - j, 0)
            )
            ref, f = y_extra[j]
            ref[f, 0:SIDE, INNER:LANES] = jnp.where(
                tile_lane < 64, shift(eby[1], -16 * j, 1), shift(eby[0], 112 - 16 * j, 1)
            )

    def pack_water(n):
        for k in range(2):
            twx[n, 0, k] = W[0, 30 + k, 0:SIDE, :]
            twx[n, 1, k] = W[0, k, 0:SIDE, :]
            twy[n, 0, k] = flat[line(0, 30 + k), :]
            twy[n, 1, k] = flat[line(0, k), :]

    def unpack_water(n):
        for k in range(2):
            W[0, 34 + k, 0:SIDE, :] = rwx[n, 0, k]
            W[0, 32 + k, 0:SIDE, :] = rwx[n, 1, k]
            flat[line(0, 38 + k), :] = rwy[n, 0, k]
            flat[line(0, 32 + k), :] = rwy[n, 1, k]

    def pack_first_water():
        for k, (fx, fy) in enumerate(((1, 2), (4, 4))):
            swx[0, k] = W[fx, 31, 0:SIDE, :]
            swx[1, k] = W[fx, 0, 0:SIDE, :]
            swy[0, k] = flat[line(fy, 31), :]
            swy[1, k] = flat[line(fy, 0), :]

    def unpack_first_water():
        for k, (fx, fy) in enumerate(((1, 2), (4, 4))):
            W[fx, 35, 0:SIDE, :] = ewx[0, k]
            W[fx, 32, 0:SIDE, :] = ewx[1, k]
            flat[line(fy, 39), :] = ewy[0, k]
            flat[line(fy, 32), :] = ewy[1, k]

    slab = ((B, 9), (G, 0), (G, 1), (G, 2), (G, 4), (CF, 7))

    def to_slab(field):
        ref, f = slab[field]
        for t in range(4):
            value = jnp.zeros((SIDE, 128), F32)
            for j in range(8):
                moved = shift(flat[line(field, 8 * t + j), :], 16 * j, 1)
                value = jnp.where(tile_lane // 16 == j, moved, value)
            ref[f, 0:SIDE, 128 * t:128 * t + 128] = value

    def from_slab(field):
        ref, f = slab[field]
        for t in range(4):
            value = ref[f, 0:SIDE, 128 * t:128 * t + 128]
            for j in range(8):
                where = line(field, 8 * t + j)
                flat[where, :] = jnp.where(
                    tile_lane < 8, shift(value, -16 * j, 1), flat[where, :]
                )

    plane_lane = lane_pos((SIDE, 128))

    def rise(value):
        forward = jnp.where(plane_lane == 127, 0.0, shift(value, -1, 1))
        return forward - shift(value, 1, 1)

    def across(value, axis, amount):
        return shift(value, -amount, axis) - shift(value, amount, axis)

    def water_step():
        def velocity(x, carry):
            below = lax.rem(x + PLANES - 1, PLANES)
            p, b = W[0, x], W[4, x]
            inner_b = b[0:SIDE]
            W[1, x, 0:SIDE] -= inner_b * (W[0, x + 1, 0:SIDE] - W[0, below, 0:SIDE])
            W[2, x] -= b * across(p, 0, 1)
            W[3, x, 0:SIDE] -= inner_b * rise(p[0:SIDE])
            return carry

        lax.fori_loop(0, SIDE, velocity, 0)
        for x, above, below in ((32, 33, 31), (35, 0, 34)):
            W[1, x, 0:SIDE] -= W[4, x, 0:SIDE] * (W[0, above, 0:SIDE] - W[0, below, 0:SIDE])

        def pressure(x, carry):
            below = lax.rem(x + PLANES - 1, PLANES)
            change = W[1, x + 1, 0:SIDE] - W[1, below, 0:SIDE]
            change = change + across(W[2, x], 0, 1)[0:SIDE] + rise(W[3, x, 0:SIDE])
            W[0, x, 0:SIDE] -= W[5, x, 0:SIDE] * change
            return carry

        lax.fori_loop(0, SIDE, pressure, 0)

    def brick_step():
        def along_x(ref, f, i, width):
            sub = row_pos((8, width))
            here = ref[f, strip(i), 0:width]
            after = ref[f, strip(lax.rem(i + 1, 5)), 0:width]
            before = ref[f, strip(lax.rem(i + 4, 5)), 0:width]
            forward = shift(jnp.where(sub == 0, after, here), -1, 0)
            backward = shift(jnp.where(sub == 7, before, here), 1, 0)
            return forward - backward

        def along_z(value, depth, above, under):
            forward = jnp.where(depth == 15, above, shift(value, -1, 1))
            backward = jnp.where(depth == 0, under, shift(value, 1, 1))
            return forward - backward

        def velocity(i, carry):
            depth = lane_pos((8, LANES)) % 16
            here = strip(i)
            s = [B[3 + k, here, :] for k in range(6)]
            p = B[9, here, :]
            forcing = (
                along_x(B, 3, i, LANES) + across(s[3], 1, 16) + along_z(s[4], depth, 0.0, 0.0),
                along_x(B, 6, i, LANES) + across(s[1], 1, 16) + along_z(s[5], depth, 0.0, 0.0),
                along_x(B, 7, i, LANES) + across(s[5], 1, 16)
                + along_z(s[2], depth, -shift(p, 15, 1), 0.0),
            )
            light = G[3, here, :]
            for k in range(3):
                B[k, here, :] += light * forcing[k]
            light = G[4, here, :]
            G[0, here, :] -= light * along_x(B, 9, i, LANES)
            G[1, here, :] -= light * across(p, 1, 16)
            G[2, here, :] -= light * (
                shift(p, -1, 1) - jnp.where(depth == 0, -shift(s[2], -15, 1), shift(p, 1, 1))
            )
            return carry

        lax.fori_loop(0, 5, velocity, 0)

        def stress(i, carry):
            depth = lane_pos((8, INNER)) % 16
            here = strip(i)
            v = [B[k, here, 0:INNER] for k in range(3)]
            dx = [along_x(B, k, i, INNER) for k in range(3)]
            dy = [across(B[k, here, :], 1, 16)[:, 0:INNER] for k in range(3)]
            dz = [
                along_z(v[k], depth, shift(G[k, here, 0:INNER], 15, 1), 0.0) for k in range(3)
            ]
            w = G[2, here, 0:INNER]
            change = along_x(G, 0, i, INNER) + across(G[1, here, :], 1, 16)[:, 0:INNER]
            change = change + shift(w, -1, 1)
            change = change - jnp.where(depth == 0, shift(v[2], -15, 1), shift(w, 1, 1))
            B[9, here, 0:INNER] -= CF[7, here, :] * change
            strain = (
                dx[0], dy[1], dz[2],
                0.5 * (dy[0] + dx[1]), 0.5 * (dz[0] + dx[2]), 0.5 * (dz[1] + dy[2]),
            )
            dilation = dx[0] + dy[1] + dz[2]
            for k in range(6):
                gain = CF[1, here, :] * strain[k]
                relaxed = CF[6, here, :] * strain[k]
                if k < 3:
                    gain = gain + CF[0, here, :] * dilation
                    relaxed = relaxed + CF[5, here, :] * dilation
                for mechanism in range(3):
                    held = M[6 * mechanism + k, here, :]
                    held = relaxed + CF[2 + mechanism, here, :] * (held - relaxed)
                    M[6 * mechanism + k, here, :] = held
                    gain = gain - held
                B[3 + k, here, 0:INNER] += gain
            return carry

        lax.fori_loop(0, 4, stress, 0)

    loads[0].wait()
    for field in range(4):
        to_slab(field)
    pack_water(0)
    count = partners[0].astype(jnp.int32)
    for there in partners[1:]:
        count = count + there.astype(jnp.int32)
    pl.semaphore_wait(barrier, count)
    start(water_copies(0))
    loads[1].wait()

    def water_params(x, carry):
        kinds = WM[x]
        W[4, x, 0:SIDE] = 0.5 * pick(kinds, table, 0)
        W[5, x, 0:SIDE] = 0.5 * pick(kinds, table, 1)
        return carry

    lax.fori_loop(0, SIDE, water_params, 0)
    pack_first_water()
    start(first_water_copies())
    to_slab(4)
    to_slab(5)
    for load in loads[2:]:
        load.wait()
    live = [live_in[s].astype(F32) for s in range(4)]

    def brick_params(i, carry):
        here = strip(i)
        lane = lane_pos((8, INNER))
        first = jnp.where(i < 2, live[0], live[2])
        second = jnp.where(i < 2, live[1], live[3])
        alive = jnp.where(lane < 256, first, second)
        kinds = MAT[here, :]
        G[3, here, 0:INNER] = 0.5 * alive * pick(kinds, table, 0)
        CF[0, here, :] = 0.5 * alive * pick(kinds, table, 1)
        CF[1, here, :] = alive * pick(kinds, table, 2)
        for mechanism in range(3):
            CF[2 + mechanism, here, :] = pick(kinds, table, 3 + mechanism)
        CF[5, here, :] = 0.5 * alive * pick(kinds, table, 6)
        CF[6, here, :] = alive * pick(kinds, table, 7)
        for k in range(9):
            B[k, here, 0:INNER] = B[k, here, 0:INNER] * alive
        for k in range(18):
            M[k, here, :] = M[k, here, :] * alive
        return carry

    lax.fori_loop(0, 4, brick_params, 0)
    pack_brick(0)
    pack_first_brick()
    start(brick_copies(0))
    start(first_brick_copies())
    arrive(first_water_copies())
    unpack_first_water()

    def step(n, carry):
        arrive(water_copies(n))
        unpack_water(n)
        water_step()

        @pl.when(n < STEPS - 1)
        def _():
            pack_water(n + 1)
            start(water_copies(n + 1))

        @pl.when(n == 0)
        def _():
            arrive(first_brick_copies())
            unpack_first_brick()

        arrive(brick_copies(n))
        unpack_brick(n)
        brick_step()

        @pl.when(n < STEPS - 1)
        def _():
            pack_brick(n + 1)
            start(brick_copies(n + 1))

        return carry

    lax.fori_loop(0, STEPS, step, 0)

    stores = []
    for s in range(4):
        rows, lanes = pl.ds(EDGE * (s // 2), EDGE), pl.ds(256 * (s % 2), 256)
        stores.append(
            pltpu.make_async_copy(
                B.at[pl.ds(0, 9), rows, lanes], motion_out.at[s], load_sem.at[2 + s]
            )
        )
        stores.append(
            pltpu.make_async_copy(M.at[:, rows, lanes], memory_out.at[s], load_sem.at[6 + s])
        )
    for store in stores:
        store.start()
    for field in range(4):
        from_slab(field)
    water_store = pltpu.make_async_copy(
        W.at[pl.ds(0, 4), pl.ds(0, SIDE), pl.ds(0, SIDE)], water_out, load_sem.at[0]
    )
    water_store.start()
    sent(first_water_copies())
    sent(first_brick_copies())
    for n in range(STEPS):
        sent(water_copies(n))
        sent(brick_copies(n))
    for store in stores:
        store.wait()
    water_store.wait()


def body(*args):
    any_space = pl.BlockSpec(memory_space=pl.ANY)
    smem = pl.BlockSpec(memory_space=pltpu.SMEM)
    messages = [
        (STEPS, 2, EDGE, INNER), (STEPS, 2, SIDE, 256), (STEPS, 4, 8, 128),
        (STEPS, 2, 2, SIDE, 128), (STEPS, 2, 2, SIDE, 128),
        (2, 8, INNER), (2, SIDE, 128), (2, 2, SIDE, 128), (2, 2, SIDE, 128),
    ]
    messages = [pltpu.VMEM(shape, F32) for shape in messages]
    return pl.pallas_call(
        kernel,
        out_shape=(
            jax.ShapeDtypeStruct((4, 9, EDGE, 256), F32),
            jax.ShapeDtypeStruct((4, 18, EDGE, 256), F32),
            jax.ShapeDtypeStruct((4, SIDE, SIDE, 128), F32),
        ),
        in_specs=[any_space, any_space, any_space, smem, any_space, any_space, smem],
        out_specs=(any_space, any_space, any_space),
        scratch_shapes=[
            pltpu.VMEM((10, ROWS, LANES), F32),
            pltpu.VMEM((5, ROWS, LANES), F32),
            pltpu.VMEM((8, SIDE, INNER), F32),
            pltpu.VMEM((18, SIDE, INNER), F32),
            pltpu.VMEM((SIDE, INNER), jnp.int32),
            pltpu.VMEM((6, PLANES, ROWS, 128), F32),
            pltpu.VMEM((SIDE, SIDE, 128), jnp.int32),
            *messages,
            *messages,
            pltpu.SemaphoreType.DMA((14,)),
            pltpu.SemaphoreType.DMA((STEPS, 12)),
            pltpu.SemaphoreType.DMA((STEPS, 12)),
            pltpu.SemaphoreType.DMA((8,)),
            pltpu.SemaphoreType.DMA((8,)),
        ],
        compiler_params=pltpu.CompilerParams(
            collective_id=0, has_side_effects=True, vmem_limit_bytes=60 << 20
        ),
        name="ultrasound_steps",
    )(*args)


def solution(mesh):
    return jax.shard_map(
        body,
        mesh=mesh,
        in_specs=(
            P(("row", "col"), None, None, None),
            P(("row", "col"), None, None, None),
            P(("row", "col"), None, None),
            P(("row", "col")),
            P(None, "row", "col", None),
            P("row", "col", None),
            P(),
        ),
        out_specs=(
            P(("row", "col"), None, None, None),
            P(("row", "col"), None, None, None),
            P(None, "row", "col", None),
        ),
        check_vma=False,
    )
```

```python
import jax
import jax.numpy as jnp
from jax import lax
from jax.experimental import pallas as pl
from jax.experimental.pallas import tpu as pltpu
from jax.sharding import PartitionSpec as P

STEPS = 3
SIDE = 32
EDGE = 16
PLANES = 36
DEEP = 56
ROWS = 40
PADDED = 40
MAIN_VMEM = 56_000_000
LANES = 640
INNER = 512
MESH = pl.DeviceIdType.MESH
F32 = jnp.float32


def lane_pos(shape):
    return lax.broadcasted_iota(jnp.int32, shape, len(shape) - 1)


def row_pos(shape):
    return lax.broadcasted_iota(jnp.int32, shape, len(shape) - 2)


def shift(value, amount, axis):
    amount = amount % value.shape[axis]
    return value if amount == 0 else pltpu.roll(value, amount, axis)


def across(value, axis, amount):
    return shift(value, -amount, axis) - shift(value, amount, axis)


def pick(indices, table, column):
    bits = [(indices & (1 << bit)) != 0 for bit in range(3)]
    values = [table[level, column] for level in range(8)]
    values = [jnp.where(bits[0], values[2 * i + 1], values[2 * i]) for i in range(4)]
    values = [jnp.where(bits[1], values[2 * i + 1], values[2 * i]) for i in range(2)]
    return jnp.where(bits[2], values[1], values[0])


def rows_of(i):
    return slice(8 * i, 8 * i + 8)


def along_x(ref, f, i, width):
    sub = row_pos((8, width))
    here = ref[f, rows_of(i), 0:width]
    after = ref[f, rows_of((i + 1) % 5), 0:width]
    before = ref[f, rows_of((i + 4) % 5), 0:width]
    forward = shift(jnp.where(sub == 0, after, here), -1, 0)
    backward = shift(jnp.where(sub == 7, before, here), 1, 0)
    return forward - backward


def along_z(value, depth, above):
    forward = jnp.where(depth == 15, above, shift(value, -1, 1))
    backward = jnp.where(depth == 0, 0.0, shift(value, 1, 1))
    return forward - backward


def brick_velocity(i, V, S, G, L, V_to, G_to):
    depth = lane_pos((8, LANES)) % 16
    here = rows_of(i)
    s = [S[k, here, :] for k in range(6)]
    p = S[6, here, :]
    light = L[0, here, :]
    V_to[0, here, :] = V[0, here, :] + light * (
        along_x(S, 0, i, LANES) + across(s[3], 1, 16) + along_z(s[4], depth, 0.0)
    )
    V_to[1, here, :] = V[1, here, :] + light * (
        along_x(S, 3, i, LANES) + across(s[1], 1, 16) + along_z(s[5], depth, 0.0)
    )
    V_to[2, here, :] = V[2, here, :] + light * (
        along_x(S, 4, i, LANES) + across(s[5], 1, 16)
        + along_z(s[2], depth, -shift(p, 15, 1))
    )
    light = L[1, here, :]
    G_to[0, here, :] = G[0, here, :] - light * along_x(S, 6, i, LANES)
    G_to[1, here, :] = G[1, here, :] - light * across(p, 1, 16)
    G_to[2, here, :] = G[2, here, :] - light * (
        shift(p, -1, 1) - jnp.where(depth == 0, -shift(s[2], -15, 1), shift(p, 1, 1))
    )


def brick_stress(i, V, S, G, CF, M, S_to, M_to):
    depth = lane_pos((8, INNER)) % 16
    here = rows_of(i)
    v = [V[k, here, 0:INNER] for k in range(3)]
    w = G[2, here, 0:INNER]
    change = along_x(G, 0, i, INNER) + across(G[1, here, :], 1, 16)[:, 0:INNER]
    change = change + shift(w, -1, 1)
    change = change - jnp.where(depth == 0, shift(v[2], -15, 1), shift(w, 1, 1))
    S_to[6, here, 0:INNER] = S[6, here, 0:INNER] - CF[7, here, :] * change
    dx = [along_x(V, k, i, INNER) for k in range(3)]
    dy = [across(V[k, here, :], 1, 16)[:, 0:INNER] for k in range(3)]
    dz = [along_z(v[k], depth, shift(G[k, here, 0:INNER], 15, 1)) for k in range(3)]
    strain = (
        dx[0], dy[1], dz[2],
        0.5 * (dy[0] + dx[1]), 0.5 * (dz[0] + dx[2]), 0.5 * (dz[1] + dy[2]),
    )
    dilation = dx[0] + dy[1] + dz[2]
    for k in range(6):
        gain = CF[1, here, :] * strain[k]
        relaxed = CF[6, here, :] * strain[k]
        if k < 3:
            gain = gain + CF[0, here, :] * dilation
            relaxed = relaxed + CF[5, here, :] * dilation
        for mechanism in range(3):
            held = M[6 * mechanism + k, here, :]
            held = relaxed + CF[2 + mechanism, here, :] * (held - relaxed)
            M_to[6 * mechanism + k, here, :] = held
            gain = gain - held
        S_to[k, here, 0:INNER] = S[k, here, 0:INNER] + gain


def main_kernel(
    mvs_in, mem_in, mat_in, live_in, water_in, wmat_in, table,
    V, S, G, L, CF, M, PR, U,
    C, MAT, WS, WM,
    tbx, tby, tbc, twx, twy, sbx, sby, swx, swy,
    rbx, rby, rbc, rwx, rwy, ebx, eby, ewx, ewy,
    load_sem, send_sem, recv_sem, xsend_sem, xrecv_sem,
):
    row, col = lax.axis_index("row"), lax.axis_index("col")
    nrow, ncol = lax.axis_size("row"), lax.axis_size("col")
    row_to = (row < nrow - 1, row > 0)
    row_from = (row > 0, row < nrow - 1)
    col_to = (col < ncol - 1, col > 0)
    col_from = (col > 0, col < ncol - 1)
    step_of = (1, -1)
    inner = pl.ds(8, SIDE)

    def line(field, y):
        return pl.ds(field * PLANES * DEEP + 2 * DEEP + 8 + y, SIDE, stride=DEEP)

    flat_p = PR.reshape(PLANES * DEEP, 128)
    flat_u = U.reshape(3 * PLANES * DEEP, 128)
    flat_c = C.reshape(3 * PLANES * DEEP, 128)
    flat_m = WM.reshape(SIDE * PADDED, 128)

    loads, motion_loads, memory_loads = [], [], []
    for s in range(4):
        rows, lanes = pl.ds(EDGE * (s // 2), EDGE), pl.ds(256 * (s % 2), 256)
        motion_loads += [
            pltpu.make_async_copy(
                mvs_in.at[s, pl.ds(0, 3)], V.at[:, rows, lanes], load_sem.at[s]
            ),
            pltpu.make_async_copy(
                mvs_in.at[s, pl.ds(3, 6)], S.at[pl.ds(0, 6), rows, lanes], load_sem.at[4 + s]
            ),
            pltpu.make_async_copy(mat_in.at[s], MAT.at[rows, lanes], load_sem.at[8 + s]),
        ]
        memory_loads.append(
            pltpu.make_async_copy(mem_in.at[s], M.at[:, rows, lanes], load_sem.at[12 + s])
        )
    pressure_load = pltpu.make_async_copy(
        water_in.at[0], PR.at[pl.ds(2, SIDE), inner], load_sem.at[16]
    )
    velocity_load = pltpu.make_async_copy(
        water_in.at[pl.ds(1, 3)], U.at[:, pl.ds(2, SIDE), inner], load_sem.at[17]
    )
    kind_load = pltpu.make_async_copy(
        wmat_in, WM.at[:, pl.ds(0, SIDE)], load_sem.at[18]
    )
    for load in motion_loads + [pressure_load, velocity_load, kind_load] + memory_loads:
        load.start()

    barrier = pltpu.get_barrier_semaphore()
    partners = []
    for dr in (-1, 0, 1):
        for dc in (-1, 0, 1):
            if dr or dc:
                there = jnp.logical_and(
                    jnp.logical_and(row + dr >= 0, row + dr < nrow),
                    jnp.logical_and(col + dc >= 0, col + dc < ncol),
                )
                partners.append(there)

                @pl.when(there)
                def _():
                    pl.semaphore_signal(
                        barrier, inc=1, device_id=(row + dr, col + dc), device_id_type=MESH
                    )

    for t in range(2):

        @pl.when(jnp.logical_not(row_from[t]))
        def _():
            rbx[:, t] = jnp.zeros((STEPS, EDGE, INNER), F32)
            rwx[:, t] = jnp.zeros((STEPS, 2, SIDE, 128), F32)
            ebx[t] = jnp.zeros((8, INNER), F32)
            ewx[t] = jnp.zeros((2, SIDE, 128), F32)

        @pl.when(jnp.logical_not(col_from[t]))
        def _():
            rby[:, t] = jnp.zeros((STEPS, SIDE, 256), F32)
            rwy[:, t] = jnp.zeros((STEPS, 2, SIDE, 128), F32)
            eby[t] = jnp.zeros((SIDE, 128), F32)
            ewy[t] = jnp.zeros((2, SIDE, 128), F32)

        for u in range(2):

            @pl.when(jnp.logical_not(jnp.logical_and(row_from[t], col_from[u])))
            def _():
                rbc[:, 2 * t + u] = jnp.zeros((STEPS, 8, 128), F32)

    def remote(src, dst, send, recv, dr, dc):
        return pltpu.make_async_remote_copy(
            src_ref=src, dst_ref=dst, send_sem=send, recv_sem=recv,
            device_id=(row + dr, col + dc), device_id_type=MESH,
        )

    def brick_x_copies(n):
        out = []
        for t in range(2):
            d = step_of[t]
            out.append((
                remote(tbx.at[n, t], rbx.at[n, t], send_sem.at[n, t], recv_sem.at[n, t], d, 0),
                row_to[t], row_from[t],
            ))
            for u in range(2):
                q = 2 * t + u
                out.append((
                    remote(tbc.at[n, q], rbc.at[n, q], send_sem.at[n, 4 + q],
                           recv_sem.at[n, 4 + q], d, step_of[u]),
                    jnp.logical_and(row_to[t], col_to[u]),
                    jnp.logical_and(row_from[t], col_from[u]),
                ))
        return out

    def side_copies(x_refs, y_refs, x_sems, y_sems):
        out = []
        for t in range(2):
            d = step_of[t]
            if x_refs:
                out.append((
                    remote(x_refs[0].at[t], x_refs[1].at[t], x_sems[0](t), x_sems[1](t), d, 0),
                    row_to[t], row_from[t],
                ))
            if y_refs:
                out.append((
                    remote(y_refs[0].at[t], y_refs[1].at[t], y_sems[0](t), y_sems[1](t), 0, d),
                    col_to[t], col_from[t],
                ))
        return out

    def step_sems(n, first):
        return (lambda t: send_sem.at[n, first + t]), (lambda t: recv_sem.at[n, first + t])

    def extra_sems(first):
        return (lambda t: xsend_sem.at[first + t]), (lambda t: xrecv_sem.at[first + t])

    def brick_y_copies(n):
        return side_copies(None, (tby.at[n], rby.at[n]), None, step_sems(n, 2))

    def water_copies(n):
        return side_copies(
            (twx.at[n], rwx.at[n]), (twy.at[n], rwy.at[n]), step_sems(n, 8), step_sems(n, 10)
        )

    def first_water_copies():
        return side_copies((swx, ewx), (swy, ewy), extra_sems(0), extra_sems(2))

    def first_brick_copies():
        return side_copies((sbx, ebx), (sby, eby), extra_sems(4), extra_sems(6))

    def start(copies):
        for copy, to, _ in copies:

            @pl.when(to)
            def _():
                copy.start()

    def arrive(copies):
        for copy, _, came in copies:

            @pl.when(came)
            def _():
                copy.wait_recv()

    def sent(copies):
        for copy, to, _ in copies:

            @pl.when(to)
            def _():
                copy.wait_send()

    pair = row_pos((8, INNER))
    tile_lane = lane_pos((SIDE, 128))
    lane, sub = lane_pos((8, 128)), row_pos((8, 128))

    def pack_brick_x(n):
        for half in range(2):
            down, up = jnp.zeros((8, INNER), F32), jnp.zeros((8, INNER), F32)
            for j in range(3 if half else 4):
                k = 4 * half + j
                here = pair // 2 == j
                up = jnp.where(here, shift(S[k, 24:32, 0:INNER], 2 * j - 6, 0), up)
                down = jnp.where(here, shift(S[k, 0:8, 0:INNER], 2 * j, 0), down)
            tbx[n, 0, 8 * half:8 * half + 8, :] = up
            tbx[n, 1, 8 * half:8 * half + 8, :] = down
        for t in range(2):
            rows = slice(24, 32) if t == 0 else slice(0, 8)
            for u in range(2):
                corner = jnp.zeros((8, 128), F32)
                for k in range(6):
                    tile = S[k, rows, 384:512] if u == 0 else S[k, rows, 0:128]
                    tile = shift(tile, 16 * k - (112 if u == 0 else 0), 1)
                    corner = jnp.where(lane // 16 == k, tile, corner)
                tbc[n, 2 * t + u] = corner

    def pack_brick_y(n):
        for half in range(2):
            ahead, back = jnp.zeros((SIDE, 128), F32), jnp.zeros((SIDE, 128), F32)
            for j in range(3 if half else 4):
                k = 4 * half + j
                here = tile_lane // 32 == j
                ahead = jnp.where(here, shift(S[k, 0:SIDE, 384:512], 32 * j - 96, 1), ahead)
                back = jnp.where(here, shift(S[k, 0:SIDE, 0:128], 32 * j, 1), back)
            tby[n, 0, :, 128 * half:128 * half + 128] = ahead
            tby[n, 1, :, 128 * half:128 * half + 128] = back

    def unpack_brick_x(n):
        for k in range(7):
            tile, j = k // 4, k % 4
            rows = rows_of(tile)
            before = shift(rbx[n, 0, rows, :], 6 - 2 * j, 0)
            after = shift(rbx[n, 1, rows, :], -2 * j, 0)
            S[k, 32:40, 0:INNER] = jnp.where(pair < 4, after, before)
        for k in range(6):
            top = jnp.where(
                lane < 64, shift(rbc[n, 3], -16 * k, 1), shift(rbc[n, 2], 112 - 16 * k, 1)
            )
            bottom = jnp.where(
                lane < 64, shift(rbc[n, 1], -16 * k, 1), shift(rbc[n, 0], 112 - 16 * k, 1)
            )
            S[k, 32:40, INNER:LANES] = jnp.where(sub < 4, top, bottom)

    def unpack_brick_y(n):
        for k in range(7):
            tile, j = k // 4, k % 4
            lanes = slice(128 * tile, 128 * tile + 128)
            before = shift(rby[n, 0, :, lanes], 96 - 32 * j, 1)
            after = shift(rby[n, 1, :, lanes], -32 * j, 1)
            S[k, 0:SIDE, INNER:LANES] = jnp.where(tile_lane < 64, after, before)

    x_extra = ((V, 0), (V, 1), (V, 2), (L, 0), (G, 0), (L, 1))
    y_extra = ((V, 0), (V, 1), (V, 2), (L, 0), (G, 1), (L, 1))

    def pack_first_brick():
        down, up = jnp.zeros((8, INNER), F32), jnp.zeros((8, INNER), F32)
        ahead, back = jnp.zeros((SIDE, 128), F32), jnp.zeros((SIDE, 128), F32)
        for j in range(6):
            ref, f = x_extra[j]
            up = jnp.where(pair == j, shift(ref[f, 24:32, 0:INNER], j - 7, 0), up)
            down = jnp.where(pair == j, shift(ref[f, 0:8, 0:INNER], j, 0), down)
            ref, f = y_extra[j]
            here = tile_lane // 16 == j
            ahead = jnp.where(here, shift(ref[f, 0:SIDE, 384:512], 16 * j - 112, 1), ahead)
            back = jnp.where(here, shift(ref[f, 0:SIDE, 0:128], 16 * j, 1), back)
        sbx[0], sbx[1], sby[0], sby[1] = up, down, ahead, back

    def unpack_first_brick():
        for j in range(6):
            ref, f = x_extra[j]
            ref[f, 32:40, 0:INNER] = jnp.where(
                pair < 4, shift(ebx[1], -j, 0), shift(ebx[0], 7 - j, 0)
            )
            ref, f = y_extra[j]
            ref[f, 0:SIDE, INNER:LANES] = jnp.where(
                tile_lane < 64, shift(eby[1], -16 * j, 1), shift(eby[0], 112 - 16 * j, 1)
            )

    def pack_water(n):
        for k in range(2):
            twx[n, 0, k] = PR[32 + k, inner, :]
            twx[n, 1, k] = PR[2 + k, inner, :]
            twy[n, 0, k] = flat_p[line(0, 30 + k), :]
            twy[n, 1, k] = flat_p[line(0, k), :]

    def unpack_water(n):
        for k in range(2):
            PR[k, inner, :] = rwx[n, 0, k]
            PR[34 + k, inner, :] = rwx[n, 1, k]
            flat_p[line(0, k - 2), :] = rwy[n, 0, k]
            flat_p[line(0, 32 + k), :] = rwy[n, 1, k]

    def pack_first_water():
        swx[0, 0], swx[0, 1] = U[0, 33, inner, :], C[0, 33, inner, :]
        swx[1, 0], swx[1, 1] = U[0, 2, inner, :], C[0, 2, inner, :]
        swy[0, 0], swy[0, 1] = flat_u[line(1, 31), :], flat_c[line(0, 31), :]
        swy[1, 0], swy[1, 1] = flat_u[line(1, 0), :], flat_c[line(0, 0), :]

    def unpack_first_water():
        U[0, 1, inner, :], C[0, 1, inner, :] = ewx[0, 0], ewx[0, 1]
        U[0, 34, inner, :], C[0, 34, inner, :] = ewx[1, 0], ewx[1, 1]
        flat_u[line(1, -1), :], flat_c[line(0, -1), :] = ewy[0, 0], ewy[0, 1]
        flat_u[line(1, 32), :], flat_c[line(0, 32), :] = ewy[1, 0], ewy[1, 1]

    def to_slab(ref, f, rows_at):
        for t in range(4):
            value = rows_at(8 * t)
            for j in range(1, 8):
                moved = shift(rows_at(8 * t + j), 16 * j, 1)
                value = jnp.where(tile_lane // 16 == j, moved, value)
            if f is None:
                ref[:, 128 * t:128 * t + 128] = value
            else:
                ref[f, 0:SIDE, 128 * t:128 * t + 128] = value

    plane_lane = lane_pos((SIDE, 128))
    wide, above_rows, below_rows = pl.ds(7, 40), pl.ds(8, 40), pl.ds(6, 40)

    def water_step():
        def velocity(x, carry):
            for plane in range(4):
                x_at = 4 * x + (2 + plane)
                p, light = PR[x_at, inner], C[0, x_at, inner]
                U[0, x_at, inner] -= light * (PR[x_at + 1, inner] - PR[x_at - 1, inner])
                U[1, x_at, wide] -= C[0, x_at, wide] * (
                    PR[x_at, above_rows] - PR[x_at, below_rows]
                )
                U[2, x_at, inner] -= C[2, x_at, inner] * (
                    jnp.where(plane_lane == 0, 0.0, p) - shift(p, 2, 1)
                )
            return carry

        lax.fori_loop(0, SIDE // 4, velocity, 0)
        for x_at in (1, 34):
            U[0, x_at, inner] -= C[0, x_at, inner] * (
                PR[x_at + 1, inner] - PR[x_at - 1, inner]
            )

        def pressure(x, carry):
            for plane in range(4):
                x_at = 4 * x + (2 + plane)
                change = U[0, x_at + 1, inner] - U[0, x_at - 1, inner]
                change = change + (U[1, x_at, pl.ds(9, SIDE)] - U[1, x_at, pl.ds(7, SIDE)])
                w = U[2, x_at, inner]
                change = change + (jnp.where(plane_lane == 127, 0.0, shift(w, -2, 1)) - w)
                PR[x_at, inner] -= C[1, x_at, inner] * change
            return carry

        lax.fori_loop(0, SIDE // 4, pressure, 0)

    for load in motion_loads:
        load.wait()
    live = [live_in[s].astype(F32) for s in range(4)]

    def alive_of(i):
        left = lane_pos((8, INNER)) < 256
        return jnp.where(
            left, jnp.where(i < 2, live[0], live[2]), jnp.where(i < 2, live[1], live[3])
        )

    def strip(i):
        return pl.ds(pl.multiple_of(8 * i, 8), 8)

    def motion_start(i, carry):
        here = strip(i)
        alive = alive_of(i)
        for k in range(3):
            V[k, here, 0:INNER] = V[k, here, 0:INNER] * alive
        for k in range(6):
            S[k, here, 0:INNER] = S[k, here, 0:INNER] * alive
        L[0, here, 0:INNER] = 0.5 * alive * pick(MAT[here, :], table, 0)
        return carry

    lax.fori_loop(0, 4, motion_start, 0)
    pressure_load.wait()
    to_slab(S, 6, lambda y: flat_p[line(0, y), :])
    pack_brick_x(0)
    pack_brick_y(0)
    count = partners[0].astype(jnp.int32)
    for there in partners[1:]:
        count = count + there.astype(jnp.int32)
    pl.semaphore_wait(barrier, count)
    start(brick_x_copies(0))
    start(brick_y_copies(0))
    velocity_load.wait()
    kind_load.wait()
    to_slab(G, 0, lambda y: flat_u[line(0, y), :])
    to_slab(G, 1, lambda y: flat_u[line(1, y), :])
    to_slab(WS, None, lambda y: flat_m[pl.ds(y, SIDE, stride=PADDED), :])

    def slab_params(i, carry):
        here = strip(i)
        L[1, here, 0:INNER] = 0.5 * pick(WS[here, :], table, 0)
        CF[7, here, :] = 0.5 * pick(WS[here, :], table, 1)
        return carry

    lax.fori_loop(0, 4, slab_params, 0)
    pack_first_brick()
    start(first_brick_copies())
    pack_water(0)
    start(water_copies(0))
    to_slab(G, 2, lambda y: flat_u[line(2, y), :])

    def water_params(x, carry):
        for plane in range(2):
            kinds = WM[2 * x + plane, 0:SIDE]
            x_at = 2 * x + (2 + plane)
            light = 0.5 * pick(kinds, table, 0)
            C[0, x_at, inner] = light
            C[1, x_at, inner] = 0.5 * pick(kinds, table, 1)
            C[2, x_at, inner] = shift(light, 1, 1)
            U[2, x_at, inner] = shift(U[2, x_at, inner], 1, 1)
        return carry

    lax.fori_loop(0, SIDE // 2, water_params, 0)
    pack_first_water()
    start(first_water_copies())
    for load in memory_loads:
        load.wait()

    def memory_start(i, carry):
        here = strip(i)
        alive = alive_of(i)
        kinds = MAT[here, :]
        CF[0, here, :] = 0.5 * alive * pick(kinds, table, 1)
        CF[1, here, :] = alive * pick(kinds, table, 2)
        for mechanism in range(3):
            CF[2 + mechanism, here, :] = pick(kinds, table, 3 + mechanism)
        CF[5, here, :] = 0.5 * alive * pick(kinds, table, 6)
        CF[6, here, :] = alive * pick(kinds, table, 7)
        for k in range(18):
            M[k, here, :] = M[k, here, :] * alive
        return carry

    lax.fori_loop(0, 4, memory_start, 0)
    arrive(first_water_copies())
    unpack_first_water()

    def step(n, carry):
        arrive(water_copies(n))
        unpack_water(n)
        water_step()
        pack_water(n + 1)
        start(water_copies(n + 1))

        @pl.when(n == 0)
        def _():
            arrive(first_brick_copies())
            unpack_first_brick()

        arrive(brick_y_copies(n))
        unpack_brick_y(n)
        for i in (1, 2):
            brick_velocity(i, V, S, G, L, V, G)
        arrive(brick_x_copies(n))
        unpack_brick_x(n)
        for i in (0, 3, 4):
            brick_velocity(i, V, S, G, L, V, G)
        for i in (0, 3):
            brick_stress(i, V, S, G, CF, M, S, M)
        pack_brick_x(n + 1)
        start(brick_x_copies(n + 1))
        for i in (1, 2):
            brick_stress(i, V, S, G, CF, M, S, M)
        pack_brick_y(n + 1)
        start(brick_y_copies(n + 1))
        return carry

    lax.fori_loop(0, STEPS - 1, step, 0)
    last = STEPS - 1
    arrive(water_copies(last))
    unpack_water(last)
    water_step()

    def settle(x, carry):
        for plane in range(4):
            x_at = 4 * x + (2 + plane)
            U[2, x_at, inner] = shift(U[2, x_at, inner], -1, 1)
        return carry

    lax.fori_loop(0, SIDE // 4, settle, 0)
    sent(first_water_copies())
    sent(first_brick_copies())
    for n in range(STEPS):
        sent(water_copies(n))
        sent(brick_x_copies(n))
        sent(brick_y_copies(n))
    arrive(brick_y_copies(last))
    unpack_brick_y(last)
    arrive(brick_x_copies(last))
    unpack_brick_x(last)


def last_kernel(
    V, S, G, L, CF, M, PR, U,
    motion_out, memory_out, water_out,
    V_to, G_to, S_to, M_to, W_to, sem,
):
    for i in range(5):
        brick_velocity(i, V, S, G, L, V_to, G_to)
    for i in range(4):
        brick_stress(i, V_to, S, G_to, CF, M, S_to, M_to)
    stores = []
    for s in range(4):
        rows, lanes = pl.ds(EDGE * (s // 2), EDGE), pl.ds(256 * (s % 2), 256)
        stores += [
            pltpu.make_async_copy(
                V_to.at[:, rows, lanes], motion_out.at[s, pl.ds(0, 3)], sem.at[s]
            ),
            pltpu.make_async_copy(
                S_to.at[pl.ds(0, 6), rows, lanes], motion_out.at[s, pl.ds(3, 6)], sem.at[4 + s]
            ),
            pltpu.make_async_copy(M_to.at[:, rows, lanes], memory_out.at[s], sem.at[8 + s]),
        ]
    for store in stores:
        store.start()
    tile_lane = lane_pos((SIDE, 128))
    flat_p = PR.reshape(PLANES * DEEP, 128)
    flat_u = U.reshape(3 * PLANES * DEEP, 128)
    flat_to = W_to.reshape(4 * SIDE * PADDED, 128)
    for field in range(4):
        ref, f = ((S_to, 6), (G_to, 0), (G_to, 1), (G_to, 2))[field]
        main = flat_p if field == 0 else flat_u
        base = 2 * DEEP + 8 + max(field - 1, 0) * PLANES * DEEP
        for t in range(4):
            value = ref[f, 0:SIDE, 128 * t:128 * t + 128]
            for j in range(8):
                y = 8 * t + j
                flat_to[pl.ds(field * SIDE * PADDED + y, SIDE, stride=PADDED), :] = jnp.where(
                    tile_lane < 8,
                    shift(value, -16 * j, 1),
                    main[pl.ds(base + y, SIDE, stride=DEEP), :],
                )
        stores.append(
            pltpu.make_async_copy(
                W_to.at[field, :, pl.ds(0, SIDE)], water_out.at[field], sem.at[12 + field]
            )
        )
        stores[-1].start()
    for store in stores:
        store.wait()


def body(*args):
    any_space = pl.BlockSpec(memory_space=pltpu.HBM)
    smem = pl.BlockSpec(memory_space=pltpu.SMEM)
    vmem = pl.BlockSpec(memory_space=pltpu.VMEM)
    messages = [
        (STEPS, 2, EDGE, INNER), (STEPS, 2, SIDE, 256), (STEPS, 4, 8, 128),
        (STEPS, 2, 2, SIDE, 128), (STEPS, 2, 2, SIDE, 128),
        (2, 8, INNER), (2, SIDE, 128), (2, 2, SIDE, 128), (2, 2, SIDE, 128),
    ]
    messages = [pltpu.VMEM(shape, F32) for shape in messages]
    state = [
        (3, ROWS, LANES), (7, ROWS, LANES), (3, ROWS, LANES), (2, ROWS, LANES),
        (8, SIDE, INNER), (18, SIDE, INNER),
        (PLANES, DEEP, 128), (3, PLANES, DEEP, 128),
    ]
    held = pl.pallas_call(
        main_kernel,
        out_shape=tuple(pltpu.VMEM(shape, F32) for shape in state),
        in_specs=[any_space, any_space, any_space, smem, any_space, any_space, smem],
        out_specs=(vmem,) * len(state),
        scratch_shapes=[
            pltpu.VMEM((3, PLANES, DEEP, 128), F32),
            pltpu.VMEM((SIDE, INNER), jnp.int32),
            pltpu.VMEM((SIDE, INNER), jnp.int32),
            pltpu.VMEM((SIDE, PADDED, 128), jnp.int32),
            *messages,
            *messages,
            pltpu.SemaphoreType.DMA((19,)),
            pltpu.SemaphoreType.DMA((STEPS, 12)),
            pltpu.SemaphoreType.DMA((STEPS, 12)),
            pltpu.SemaphoreType.DMA((8,)),
            pltpu.SemaphoreType.DMA((8,)),
        ],
        compiler_params=pltpu.CompilerParams(
            collective_id=0, has_side_effects=True, vmem_limit_bytes=MAIN_VMEM
        ),
        name="ultrasound_steps",
    )(*args)
    return pl.pallas_call(
        last_kernel,
        out_shape=(
            jax.ShapeDtypeStruct((4, 9, EDGE, 256), F32),
            jax.ShapeDtypeStruct((4, 18, EDGE, 256), F32),
            jax.ShapeDtypeStruct((4, SIDE, SIDE, 128), F32),
        ),
        in_specs=[vmem] * 8,
        out_specs=(any_space,) * 3,
        scratch_shapes=[
            pltpu.VMEM((3, ROWS, LANES), F32),
            pltpu.VMEM((3, ROWS, LANES), F32),
            pltpu.VMEM((7, SIDE, INNER), F32),
            pltpu.VMEM((18, SIDE, INNER), F32),
            pltpu.VMEM((4, SIDE, PADDED, 128), F32),
            pltpu.SemaphoreType.DMA((16,)),
        ],
        compiler_params=pltpu.CompilerParams(vmem_limit_bytes=24 << 20),
        name="ultrasound_last",
    )(*held)


def solution(mesh):
    return jax.shard_map(
        body,
        mesh=mesh,
        in_specs=(
            P(("row", "col"), None, None, None),
            P(("row", "col"), None, None, None),
            P(("row", "col"), None, None),
            P(("row", "col")),
            P(None, "row", "col", None),
            P("row", "col", None),
            P(),
        ),
        out_specs=(
            P(("row", "col"), None, None, None),
            P(("row", "col"), None, None, None),
            P(None, "row", "col", None),
        ),
        check_vma=False,
    )
```

```python
import jax
import jax.numpy as jnp
from jax import lax
from jax.experimental import pallas as pl
from jax.experimental.pallas import tpu as pltpu
from jax.sharding import PartitionSpec as P

STEPS = 3
SIDE = 32
EDGE = 16
PLANES = 36
DEEP = 56
ROWS = 40
PADDED = 40
MAIN_VMEM = 56_000_000
LANES = 640
INNER = 512
MESH = pl.DeviceIdType.MESH
F32 = jnp.float32
BF16 = jnp.bfloat16


def lane_pos(shape):
    return lax.broadcasted_iota(jnp.int32, shape, len(shape) - 1)


def row_pos(shape):
    return lax.broadcasted_iota(jnp.int32, shape, len(shape) - 2)


def shift(value, amount, axis):
    amount = amount % value.shape[axis]
    return value if amount == 0 else pltpu.roll(value, amount, axis)


def across(value, axis, amount):
    return shift(value, -amount, axis) - shift(value, amount, axis)


def pick(indices, table, column):
    bits = [(indices & (1 << bit)) != 0 for bit in range(3)]
    values = [table[level, column] for level in range(8)]
    values = [jnp.where(bits[0], values[2 * i + 1], values[2 * i]) for i in range(4)]
    values = [jnp.where(bits[1], values[2 * i + 1], values[2 * i]) for i in range(2)]
    return jnp.where(bits[2], values[1], values[0])


def rows_of(i):
    return slice(8 * i, 8 * i + 8)


def along_x(ref, f, i, width):
    sub = row_pos((8, width))
    here = ref[f, rows_of(i), 0:width]
    after = ref[f, rows_of((i + 1) % 5), 0:width]
    before = ref[f, rows_of((i + 4) % 5), 0:width]
    forward = shift(jnp.where(sub == 0, after, here), -1, 0)
    backward = shift(jnp.where(sub == 7, before, here), 1, 0)
    return forward - backward


def z_weights(W):
    k = lax.broadcasted_iota(jnp.int32, (128, 128), 0)
    at = lax.broadcasted_iota(jnp.int32, (128, 128), 1)
    depth = at % 16
    up = jnp.logical_and(k == at + 1, depth != 15).astype(F32)
    down = jnp.logical_and(k == at - 1, depth != 0).astype(F32)
    change = (up - down).astype(BF16)
    top = jnp.logical_and(k == at - 15, depth == 15).astype(F32)
    base = jnp.logical_and(k == at + 15, depth == 0).astype(F32)
    for half, sign in ((0, 1.0), (1, -1.0)):
        into_brick, into_water = (-sign * top).astype(BF16), (sign * base).astype(BF16)
        for part in range(2):
            rows = slice(128 * part, 128 * part + 128)
            W[half, rows, 0:128], W[half, rows, 128:256] = change, into_water
            rows = slice(256 + 128 * part, 384 + 128 * part)
            W[half, rows, 0:128], W[half, rows, 128:256] = into_brick, change


def parts(values):
    out = []
    for value in values:
        high = value.astype(BF16)
        out += [high, (value - high.astype(F32)).astype(BF16)]
    return jnp.concatenate(out, axis=1)


def stacked(ref, f, tiles):
    return jnp.concatenate(
        [ref[f, rows_of(i), 128 * t:128 * t + 128] for i, t in tiles], axis=0
    )


def unstacked(value, tiles, i, count):
    none = jnp.zeros((8, 128), F32)
    found = []
    for t in range(count):
        if (i, t) in tiles:
            place = 8 * tiles.index((i, t))
            found.append(value[place:place + 8])
        else:
            found.append(none)
    return jnp.concatenate(found, axis=1)


def times(values, weights):
    return jnp.dot(parts(values), weights, preferred_element_type=F32)


def brick_velocity(group, V, S, G, L, W, V_to, G_to):
    tiles = [(i, t) for i in group for t in range(5) if (i, t) != (4, 4)]
    single = W[0, 0:256, 0:128]
    xz = times([stacked(S, 4, tiles)], single)
    yz = times([stacked(S, 5, tiles)], single)
    both = times([stacked(S, 2, tiles), stacked(S, 6, tiles)], W[0])
    for i in group:
        here = rows_of(i)
        light = L[0, here, :]
        V_to[0, here, :] = V[0, here, :] + light * (
            along_x(S, 0, i, LANES) + across(S[3, here, :], 1, 16)
            + unstacked(xz, tiles, i, 5)
        )
        V_to[1, here, :] = V[1, here, :] + light * (
            along_x(S, 3, i, LANES) + across(S[1, here, :], 1, 16)
            + unstacked(yz, tiles, i, 5)
        )
        V_to[2, here, :] = V[2, here, :] + light * (
            along_x(S, 4, i, LANES) + across(S[5, here, :], 1, 16)
            + unstacked(both[:, 0:128], tiles, i, 5)
        )
        light = L[1, here, :]
        G_to[0, here, :] = G[0, here, :] - light * along_x(S, 6, i, LANES)
        G_to[1, here, :] = G[1, here, :] - light * across(S[6, here, :], 1, 16)
        G_to[2, here, :] = G[2, here, :] - light * unstacked(both[:, 128:256], tiles, i, 5)


def brick_stress(group, V, S, G, CF, M, W, S_to, M_to):
    tiles = [(i, t) for i in group for t in range(4)]
    pair = W[1, :, 0:128]
    z_all = [
        times([stacked(V, 0, tiles), stacked(G, 0, tiles)], pair),
        times([stacked(V, 1, tiles), stacked(G, 1, tiles)], pair),
    ]
    both = times([stacked(V, 2, tiles), stacked(G, 2, tiles)], W[1])
    z_all.append(both[:, 0:128])
    for i in group:
        here = rows_of(i)
        change = along_x(G, 0, i, INNER) + across(G[1, here, :], 1, 16)[:, 0:INNER]
        change = change + unstacked(both[:, 128:256], tiles, i, 4)
        S_to[6, here, 0:INNER] = S[6, here, 0:INNER] - CF[7, here, :] * change
        dx = [along_x(V, k, i, INNER) for k in range(3)]
        dy = [across(V[k, here, :], 1, 16)[:, 0:INNER] for k in range(3)]
        dz = [unstacked(z_all[k], tiles, i, 4) for k in range(3)]
        strain = (
            dx[0], dy[1], dz[2],
            0.5 * (dy[0] + dx[1]), 0.5 * (dz[0] + dx[2]), 0.5 * (dz[1] + dy[2]),
        )
        dilation = dx[0] + dy[1] + dz[2]
        for k in range(6):
            gain = CF[1, here, :] * strain[k]
            relaxed = CF[6, here, :] * strain[k]
            if k < 3:
                gain = gain + CF[0, here, :] * dilation
                relaxed = relaxed + CF[5, here, :] * dilation
            for mechanism in range(3):
                held = M[6 * mechanism + k, here, :]
                held = relaxed + CF[2 + mechanism, here, :] * (held - relaxed)
                M_to[6 * mechanism + k, here, :] = held
                gain = gain - held
            S_to[k, here, 0:INNER] = S[k, here, 0:INNER] + gain


def main_kernel(
    mvs_in, mem_in, mat_in, live_in, water_in, wmat_in, table,
    V, S, G, L, CF, M, PR, U,
    C, ZW, MAT, WS, WM,
    tbx, tby, tbc, twx, twy, sbx, sby, swx, swy,
    rbx, rby, rbc, rwx, rwy, ebx, eby, ewx, ewy,
    load_sem, send_sem, recv_sem, xsend_sem, xrecv_sem,
):
    row, col = lax.axis_index("row"), lax.axis_index("col")
    nrow, ncol = lax.axis_size("row"), lax.axis_size("col")
    row_to = (row < nrow - 1, row > 0)
    row_from = (row > 0, row < nrow - 1)
    col_to = (col < ncol - 1, col > 0)
    col_from = (col > 0, col < ncol - 1)
    step_of = (1, -1)
    inner = pl.ds(8, SIDE)

    def line(field, y):
        return pl.ds(field * PLANES * DEEP + 2 * DEEP + 8 + y, SIDE, stride=DEEP)

    flat_p = PR.reshape(PLANES * DEEP, 128)
    flat_u = U.reshape(3 * PLANES * DEEP, 128)
    flat_c = C.reshape(3 * PLANES * DEEP, 128)
    flat_m = WM.reshape(SIDE * PADDED, 128)

    loads, motion_loads, memory_loads = [], [], []
    for s in range(4):
        rows, lanes = pl.ds(EDGE * (s // 2), EDGE), pl.ds(256 * (s % 2), 256)
        motion_loads += [
            pltpu.make_async_copy(
                mvs_in.at[s, pl.ds(0, 3)], V.at[:, rows, lanes], load_sem.at[s]
            ),
            pltpu.make_async_copy(
                mvs_in.at[s, pl.ds(3, 6)], S.at[pl.ds(0, 6), rows, lanes], load_sem.at[4 + s]
            ),
            pltpu.make_async_copy(mat_in.at[s], MAT.at[rows, lanes], load_sem.at[8 + s]),
        ]
        memory_loads.append(
            pltpu.make_async_copy(mem_in.at[s], M.at[:, rows, lanes], load_sem.at[12 + s])
        )
    pressure_load = pltpu.make_async_copy(
        water_in.at[0], PR.at[pl.ds(2, SIDE), inner], load_sem.at[16]
    )
    velocity_load = pltpu.make_async_copy(
        water_in.at[pl.ds(1, 3)], U.at[:, pl.ds(2, SIDE), inner], load_sem.at[17]
    )
    kind_load = pltpu.make_async_copy(
        wmat_in, WM.at[:, pl.ds(0, SIDE)], load_sem.at[18]
    )
    for load in [pressure_load, velocity_load, kind_load] + motion_loads + memory_loads:
        load.start()

    barrier = pltpu.get_barrier_semaphore()
    partners = []
    for dr in (-1, 0, 1):
        for dc in (-1, 0, 1):
            if dr or dc:
                there = jnp.logical_and(
                    jnp.logical_and(row + dr >= 0, row + dr < nrow),
                    jnp.logical_and(col + dc >= 0, col + dc < ncol),
                )
                partners.append(there)

                @pl.when(there)
                def _():
                    pl.semaphore_signal(
                        barrier, inc=1, device_id=(row + dr, col + dc), device_id_type=MESH
                    )

    for t in range(2):

        @pl.when(jnp.logical_not(row_from[t]))
        def _():
            rbx[:, t] = jnp.zeros((STEPS, EDGE, INNER), F32)
            rwx[:, t] = jnp.zeros((STEPS, 2, SIDE, 128), F32)
            ebx[t] = jnp.zeros((8, INNER), F32)
            ewx[t] = jnp.zeros((2, SIDE, 128), F32)

        @pl.when(jnp.logical_not(col_from[t]))
        def _():
            rby[:, t] = jnp.zeros((STEPS, SIDE, 256), F32)
            rwy[:, t] = jnp.zeros((STEPS, 2, SIDE, 128), F32)
            eby[t] = jnp.zeros((SIDE, 128), F32)
            ewy[t] = jnp.zeros((2, SIDE, 128), F32)

        for u in range(2):

            @pl.when(jnp.logical_not(jnp.logical_and(row_from[t], col_from[u])))
            def _():
                rbc[:, 2 * t + u] = jnp.zeros((STEPS, 8, 128), F32)

    def remote(src, dst, send, recv, dr, dc):
        return pltpu.make_async_remote_copy(
            src_ref=src, dst_ref=dst, send_sem=send, recv_sem=recv,
            device_id=(row + dr, col + dc), device_id_type=MESH,
        )

    def brick_x_copies(n):
        out = []
        for t in range(2):
            d = step_of[t]
            out.append((
                remote(tbx.at[n, t], rbx.at[n, t], send_sem.at[n, t], recv_sem.at[n, t], d, 0),
                row_to[t], row_from[t],
            ))
            for u in range(2):
                q = 2 * t + u
                out.append((
                    remote(tbc.at[n, q], rbc.at[n, q], send_sem.at[n, 4 + q],
                           recv_sem.at[n, 4 + q], d, step_of[u]),
                    jnp.logical_and(row_to[t], col_to[u]),
                    jnp.logical_and(row_from[t], col_from[u]),
                ))
        return out

    def side_copies(x_refs, y_refs, x_sems, y_sems):
        out = []
        for t in range(2):
            d = step_of[t]
            if x_refs:
                out.append((
                    remote(x_refs[0].at[t], x_refs[1].at[t], x_sems[0](t), x_sems[1](t), d, 0),
                    row_to[t], row_from[t],
                ))
            if y_refs:
                out.append((
                    remote(y_refs[0].at[t], y_refs[1].at[t], y_sems[0](t), y_sems[1](t), 0, d),
                    col_to[t], col_from[t],
                ))
        return out

    def step_sems(n, first):
        return (lambda t: send_sem.at[n, first + t]), (lambda t: recv_sem.at[n, first + t])

    def extra_sems(first):
        return (lambda t: xsend_sem.at[first + t]), (lambda t: xrecv_sem.at[first + t])

    def brick_y_copies(n):
        return side_copies(None, (tby.at[n], rby.at[n]), None, step_sems(n, 2))

    def water_x_copies(n):
        return side_copies((twx.at[n], rwx.at[n]), None, step_sems(n, 8), None)

    def water_y_copies(n):
        return side_copies(None, (twy.at[n], rwy.at[n]), None, step_sems(n, 10))

    def first_water_copies():
        return side_copies((swx, ewx), (swy, ewy), extra_sems(0), extra_sems(2))

    def first_brick_copies():
        return side_copies((sbx, ebx), (sby, eby), extra_sems(4), extra_sems(6))

    def start(copies):
        for copy, to, _ in copies:

            @pl.when(to)
            def _():
                copy.start()

    def arrive(copies):
        for copy, _, came in copies:

            @pl.when(came)
            def _():
                copy.wait_recv()

    def sent(copies):
        for copy, to, _ in copies:

            @pl.when(to)
            def _():
                copy.wait_send()

    pair = row_pos((8, INNER))
    tile_lane = lane_pos((SIDE, 128))
    lane, sub = lane_pos((8, 128)), row_pos((8, 128))

    def pack_brick_x(n):
        for half in range(2):
            down, up = jnp.zeros((8, INNER), F32), jnp.zeros((8, INNER), F32)
            for j in range(3 if half else 4):
                k = 4 * half + j
                here = pair // 2 == j
                up = jnp.where(here, shift(S[k, 24:32, 0:INNER], 2 * j - 6, 0), up)
                down = jnp.where(here, shift(S[k, 0:8, 0:INNER], 2 * j, 0), down)
            tbx[n, 0, 8 * half:8 * half + 8, :] = up
            tbx[n, 1, 8 * half:8 * half + 8, :] = down
        for t in range(2):
            rows = slice(24, 32) if t == 0 else slice(0, 8)
            for u in range(2):
                corner = jnp.zeros((8, 128), F32)
                for k in range(6):
                    tile = S[k, rows, 384:512] if u == 0 else S[k, rows, 0:128]
                    tile = shift(tile, 16 * k - (112 if u == 0 else 0), 1)
                    corner = jnp.where(lane // 16 == k, tile, corner)
                tbc[n, 2 * t + u] = corner

    def pack_brick_y(n):
        for half in range(2):
            ahead, back = jnp.zeros((SIDE, 128), F32), jnp.zeros((SIDE, 128), F32)
            for j in range(3 if half else 4):
                k = 4 * half + j
                here = tile_lane // 32 == j
                ahead = jnp.where(here, shift(S[k, 0:SIDE, 384:512], 32 * j - 96, 1), ahead)
                back = jnp.where(here, shift(S[k, 0:SIDE, 0:128], 32 * j, 1), back)
            tby[n, 0, :, 128 * half:128 * half + 128] = ahead
            tby[n, 1, :, 128 * half:128 * half + 128] = back

    def unpack_brick_x(n):
        for k in range(7):
            tile, j = k // 4, k % 4
            rows = rows_of(tile)
            before = shift(rbx[n, 0, rows, :], 6 - 2 * j, 0)
            after = shift(rbx[n, 1, rows, :], -2 * j, 0)
            S[k, 32:40, 0:INNER] = jnp.where(pair < 4, after, before)
        for k in range(6):
            top = jnp.where(
                lane < 64, shift(rbc[n, 3], -16 * k, 1), shift(rbc[n, 2], 112 - 16 * k, 1)
            )
            bottom = jnp.where(
                lane < 64, shift(rbc[n, 1], -16 * k, 1), shift(rbc[n, 0], 112 - 16 * k, 1)
            )
            S[k, 32:40, INNER:LANES] = jnp.where(sub < 4, top, bottom)

    def unpack_brick_y(n):
        for k in range(7):
            tile, j = k // 4, k % 4
            lanes = slice(128 * tile, 128 * tile + 128)
            before = shift(rby[n, 0, :, lanes], 96 - 32 * j, 1)
            after = shift(rby[n, 1, :, lanes], -32 * j, 1)
            S[k, 0:SIDE, INNER:LANES] = jnp.where(tile_lane < 64, after, before)

    x_extra = ((V, 0), (V, 1), (V, 2), (L, 0), (G, 0), (L, 1))
    y_extra = ((V, 0), (V, 1), (V, 2), (L, 0), (G, 1), (L, 1))

    def pack_first_brick():
        down, up = jnp.zeros((8, INNER), F32), jnp.zeros((8, INNER), F32)
        ahead, back = jnp.zeros((SIDE, 128), F32), jnp.zeros((SIDE, 128), F32)
        for j in range(6):
            ref, f = x_extra[j]
            up = jnp.where(pair == j, shift(ref[f, 24:32, 0:INNER], j - 7, 0), up)
            down = jnp.where(pair == j, shift(ref[f, 0:8, 0:INNER], j, 0), down)
            ref, f = y_extra[j]
            here = tile_lane // 16 == j
            ahead = jnp.where(here, shift(ref[f, 0:SIDE, 384:512], 16 * j - 112, 1), ahead)
            back = jnp.where(here, shift(ref[f, 0:SIDE, 0:128], 16 * j, 1), back)
        sbx[0], sbx[1], sby[0], sby[1] = up, down, ahead, back

    def unpack_first_brick():
        for j in range(6):
            ref, f = x_extra[j]
            ref[f, 32:40, 0:INNER] = jnp.where(
                pair < 4, shift(ebx[1], -j, 0), shift(ebx[0], 7 - j, 0)
            )
            ref, f = y_extra[j]
            ref[f, 0:SIDE, INNER:LANES] = jnp.where(
                tile_lane < 64, shift(eby[1], -16 * j, 1), shift(eby[0], 112 - 16 * j, 1)
            )

    def pack_water_x(n):
        for k in range(2):
            twx[n, 0, k] = PR[32 + k, inner, :]
            twx[n, 1, k] = PR[2 + k, inner, :]

    def pack_water_y(n):
        for k in range(2):
            twy[n, 0, k] = flat_p[line(0, 30 + k), :]
            twy[n, 1, k] = flat_p[line(0, k), :]

    def unpack_water(n):
        for k in range(2):
            PR[k, inner, :] = rwx[n, 0, k]
            PR[34 + k, inner, :] = rwx[n, 1, k]
            flat_p[line(0, k - 2), :] = rwy[n, 0, k]
            flat_p[line(0, 32 + k), :] = rwy[n, 1, k]

    def pack_first_water():
        for t in range(2):
            end = SIDE - 1 if t == 0 else 0
            swx[t, 0] = U[0, 2 + end, inner, :]
            swx[t, 1] = 0.5 * pick(WM[end, 0:SIDE, :], table, 0)
            swy[t, 0] = flat_u[line(1, end), :]
            swy[t, 1] = 0.5 * pick(flat_m[pl.ds(end, SIDE, stride=PADDED), :], table, 0)

    def unpack_first_water():
        U[0, 1, inner, :], C[0, 1, inner, :] = ewx[0, 0], ewx[0, 1]
        U[0, 34, inner, :], C[0, 34, inner, :] = ewx[1, 0], ewx[1, 1]
        flat_u[line(1, -1), :], flat_c[line(0, -1), :] = ewy[0, 0], ewy[0, 1]
        flat_u[line(1, 32), :], flat_c[line(0, 32), :] = ewy[1, 0], ewy[1, 1]

    def to_slab(ref, f, rows_at):
        for t in range(4):
            value = rows_at(8 * t)
            for j in range(1, 8):
                moved = shift(rows_at(8 * t + j), 16 * j, 1)
                value = jnp.where(tile_lane // 16 == j, moved, value)
            if f is None:
                ref[:, 128 * t:128 * t + 128] = value
            else:
                ref[f, 0:SIDE, 128 * t:128 * t + 128] = value

    plane_lane = lane_pos((SIDE, 128))
    wide, above_rows, below_rows = pl.ds(7, 40), pl.ds(8, 40), pl.ds(6, 40)

    def x_velocity(x_at):
        U[0, x_at, inner] -= C[0, x_at, inner] * (PR[x_at + 1, inner] - PR[x_at - 1, inner])

    def water_velocity(x_at):
        x_velocity(x_at)
        U[1, x_at, wide] -= C[0, x_at, wide] * (PR[x_at, above_rows] - PR[x_at, below_rows])
        p = PR[x_at, inner]
        U[2, x_at, inner] -= C[2, x_at, inner] * (
            jnp.where(plane_lane == 0, 0.0, p) - shift(p, 2, 1)
        )

    def water_pressure(x_at):
        change = U[0, x_at + 1, inner] - U[0, x_at - 1, inner]
        change = change + (U[1, x_at, pl.ds(9, SIDE)] - U[1, x_at, pl.ds(7, SIDE)])
        w = U[2, x_at, inner]
        change = change + (jnp.where(plane_lane == 127, 0.0, shift(w, -2, 1)) - w)
        PR[x_at, inner] -= C[1, x_at, inner] * change

    def water_ends():
        x_velocity(1)
        x_velocity(34)
        for x_at in (2, 3, 4, 5, 30, 31, 32, 33):
            water_velocity(x_at)
        for x_at in (2, 3, 32, 33):
            water_pressure(x_at)

    def water_rest():
        def velocity(x, carry):
            for plane in range(4):
                water_velocity(4 * x + (6 + plane))
            return carry

        lax.fori_loop(0, 6, velocity, 0)

        def pressure(x, carry):
            for plane in range(4):
                water_pressure(4 * x + (4 + plane))
            return carry

        lax.fori_loop(0, 7, pressure, 0)

    pressure_load.wait()
    velocity_load.wait()
    kind_load.wait()
    pack_water_x(0)
    pack_water_y(0)
    pack_first_water()
    for load in motion_loads:
        load.wait()
    live = [live_in[s].astype(F32) for s in range(4)]

    def alive_of(i):
        left = lane_pos((8, INNER)) < 256
        return jnp.where(
            left, jnp.where(i < 2, live[0], live[2]), jnp.where(i < 2, live[1], live[3])
        )

    def strip(i):
        return pl.ds(pl.multiple_of(8 * i, 8), 8)

    def motion_start(i, carry):
        here = strip(i)
        alive = alive_of(i)
        for k in range(3):
            V[k, here, 0:INNER] = V[k, here, 0:INNER] * alive
        for k in range(6):
            S[k, here, 0:INNER] = S[k, here, 0:INNER] * alive
        L[0, here, 0:INNER] = 0.5 * alive * pick(MAT[here, :], table, 0)
        return carry

    lax.fori_loop(0, 4, motion_start, 0)
    to_slab(S, 6, lambda y: flat_p[line(0, y), :])
    pack_brick_x(0)
    pack_brick_y(0)
    count = partners[0].astype(jnp.int32)
    for there in partners[1:]:
        count = count + there.astype(jnp.int32)
    pl.semaphore_wait(barrier, count)
    start(water_x_copies(0))
    start(water_y_copies(0))
    start(first_water_copies())
    start(brick_x_copies(0))
    start(brick_y_copies(0))
    to_slab(G, 0, lambda y: flat_u[line(0, y), :])
    to_slab(G, 1, lambda y: flat_u[line(1, y), :])
    to_slab(WS, None, lambda y: flat_m[pl.ds(y, SIDE, stride=PADDED), :])

    def slab_params(i, carry):
        here = strip(i)
        L[1, here, 0:INNER] = 0.5 * pick(WS[here, :], table, 0)
        CF[7, here, :] = 0.5 * pick(WS[here, :], table, 1)
        return carry

    lax.fori_loop(0, 4, slab_params, 0)
    pack_first_brick()
    start(first_brick_copies())
    to_slab(G, 2, lambda y: flat_u[line(2, y), :])
    z_weights(ZW)

    def water_params(x, carry):
        for plane in range(2):
            kinds = WM[2 * x + plane, 0:SIDE]
            x_at = 2 * x + (2 + plane)
            light = 0.5 * pick(kinds, table, 0)
            C[0, x_at, inner] = light
            C[1, x_at, inner] = 0.5 * pick(kinds, table, 1)
            C[2, x_at, inner] = shift(light, 1, 1)
            U[2, x_at, inner] = shift(U[2, x_at, inner], 1, 1)
        return carry

    lax.fori_loop(0, SIDE // 2, water_params, 0)
    for load in memory_loads:
        load.wait()

    def memory_start(i, carry):
        here = strip(i)
        alive = alive_of(i)
        kinds = MAT[here, :]
        CF[0, here, :] = 0.5 * alive * pick(kinds, table, 1)
        CF[1, here, :] = alive * pick(kinds, table, 2)
        for mechanism in range(3):
            CF[2 + mechanism, here, :] = pick(kinds, table, 3 + mechanism)
        CF[5, here, :] = 0.5 * alive * pick(kinds, table, 6)
        CF[6, here, :] = alive * pick(kinds, table, 7)
        for k in range(18):
            M[k, here, :] = M[k, here, :] * alive
        return carry

    lax.fori_loop(0, 4, memory_start, 0)
    arrive(first_water_copies())
    unpack_first_water()

    def step(n, carry):
        arrive(water_y_copies(n))
        arrive(water_x_copies(n))
        unpack_water(n)
        water_ends()
        pack_water_x(n + 1)
        start(water_x_copies(n + 1))
        water_rest()
        pack_water_y(n + 1)
        start(water_y_copies(n + 1))

        @pl.when(n == 0)
        def _():
            arrive(first_brick_copies())
            unpack_first_brick()

        arrive(brick_y_copies(n))
        unpack_brick_y(n)
        brick_velocity((1, 2), V, S, G, L, ZW, V, G)
        arrive(brick_x_copies(n))
        unpack_brick_x(n)
        brick_velocity((0, 3, 4), V, S, G, L, ZW, V, G)
        brick_stress((0, 3), V, S, G, CF, M, ZW, S, M)
        pack_brick_x(n + 1)
        start(brick_x_copies(n + 1))
        brick_stress((1, 2), V, S, G, CF, M, ZW, S, M)
        pack_brick_y(n + 1)
        start(brick_y_copies(n + 1))
        return carry

    lax.fori_loop(0, STEPS - 1, step, 0)
    last = STEPS - 1
    arrive(water_y_copies(last))
    arrive(water_x_copies(last))
    unpack_water(last)
    water_ends()
    water_rest()

    def settle(x, carry):
        for plane in range(4):
            x_at = 4 * x + (2 + plane)
            U[2, x_at, inner] = shift(U[2, x_at, inner], -1, 1)
        return carry

    lax.fori_loop(0, SIDE // 4, settle, 0)
    sent(first_water_copies())
    sent(first_brick_copies())
    for n in range(STEPS):
        sent(water_x_copies(n))
        sent(water_y_copies(n))
        sent(brick_x_copies(n))
        sent(brick_y_copies(n))
    arrive(brick_y_copies(last))
    unpack_brick_y(last)
    arrive(brick_x_copies(last))
    unpack_brick_x(last)


def last_kernel(
    V, S, G, L, CF, M, PR, U,
    motion_out, memory_out, water_out,
    V_to, G_to, S_to, M_to, W_to, ZW, sem,
):
    z_weights(ZW)
    brick_velocity((0, 1, 2, 3, 4), V, S, G, L, ZW, V_to, G_to)
    brick_stress((0, 1, 2, 3), V_to, S, G_to, CF, M, ZW, S_to, M_to)
    stores = []
    for s in range(4):
        rows, lanes = pl.ds(EDGE * (s // 2), EDGE), pl.ds(256 * (s % 2), 256)
        stores += [
            pltpu.make_async_copy(
                V_to.at[:, rows, lanes], motion_out.at[s, pl.ds(0, 3)], sem.at[s]
            ),
            pltpu.make_async_copy(
                S_to.at[pl.ds(0, 6), rows, lanes], motion_out.at[s, pl.ds(3, 6)], sem.at[4 + s]
            ),
            pltpu.make_async_copy(M_to.at[:, rows, lanes], memory_out.at[s], sem.at[8 + s]),
        ]
    for store in stores:
        store.start()
    tile_lane = lane_pos((SIDE, 128))
    flat_p = PR.reshape(PLANES * DEEP, 128)
    flat_u = U.reshape(3 * PLANES * DEEP, 128)
    flat_to = W_to.reshape(4 * SIDE * PADDED, 128)
    for field in range(4):
        ref, f = ((S_to, 6), (G_to, 0), (G_to, 1), (G_to, 2))[field]
        main = flat_p if field == 0 else flat_u
        base = 2 * DEEP + 8 + max(field - 1, 0) * PLANES * DEEP
        for t in range(4):
            value = ref[f, 0:SIDE, 128 * t:128 * t + 128]
            for j in range(8):
                y = 8 * t + j
                flat_to[pl.ds(field * SIDE * PADDED + y, SIDE, stride=PADDED), :] = jnp.where(
                    tile_lane < 8,
                    shift(value, -16 * j, 1),
                    main[pl.ds(base + y, SIDE, stride=DEEP), :],
                )
        stores.append(
            pltpu.make_async_copy(
                W_to.at[field, :, pl.ds(0, SIDE)], water_out.at[field], sem.at[12 + field]
            )
        )
        stores[-1].start()
    for store in stores:
        store.wait()


def body(*args):
    any_space = pl.BlockSpec(memory_space=pltpu.HBM)
    smem = pl.BlockSpec(memory_space=pltpu.SMEM)
    vmem = pl.BlockSpec(memory_space=pltpu.VMEM)
    messages = [
        (STEPS, 2, EDGE, INNER), (STEPS, 2, SIDE, 256), (STEPS, 4, 8, 128),
        (STEPS, 2, 2, SIDE, 128), (STEPS, 2, 2, SIDE, 128),
        (2, 8, INNER), (2, SIDE, 128), (2, 2, SIDE, 128), (2, 2, SIDE, 128),
    ]
    messages = [pltpu.VMEM(shape, F32) for shape in messages]
    state = [
        (3, ROWS, LANES), (7, ROWS, LANES), (3, ROWS, LANES), (2, ROWS, LANES),
        (8, SIDE, INNER), (18, SIDE, INNER),
        (PLANES, DEEP, 128), (3, PLANES, DEEP, 128),
    ]
    held = pl.pallas_call(
        main_kernel,
        out_shape=tuple(pltpu.VMEM(shape, F32) for shape in state),
        in_specs=[any_space, any_space, any_space, smem, any_space, any_space, smem],
        out_specs=(vmem,) * len(state),
        scratch_shapes=[
            pltpu.VMEM((3, PLANES, DEEP, 128), F32),
            pltpu.VMEM((2, 512, 256), BF16),
            pltpu.VMEM((SIDE, INNER), jnp.int32),
            pltpu.VMEM((SIDE, INNER), jnp.int32),
            pltpu.VMEM((SIDE, PADDED, 128), jnp.int32),
            *messages,
            *messages,
            pltpu.SemaphoreType.DMA((19,)),
            pltpu.SemaphoreType.DMA((STEPS, 12)),
            pltpu.SemaphoreType.DMA((STEPS, 12)),
            pltpu.SemaphoreType.DMA((8,)),
            pltpu.SemaphoreType.DMA((8,)),
        ],
        compiler_params=pltpu.CompilerParams(
            collective_id=0, has_side_effects=True, vmem_limit_bytes=MAIN_VMEM
        ),
        name="ultrasound_steps",
    )(*args)
    return pl.pallas_call(
        last_kernel,
        out_shape=(
            jax.ShapeDtypeStruct((4, 9, EDGE, 256), F32),
            jax.ShapeDtypeStruct((4, 18, EDGE, 256), F32),
            jax.ShapeDtypeStruct((4, SIDE, SIDE, 128), F32),
        ),
        in_specs=[vmem] * 8,
        out_specs=(any_space,) * 3,
        scratch_shapes=[
            pltpu.VMEM((3, ROWS, LANES), F32),
            pltpu.VMEM((3, ROWS, LANES), F32),
            pltpu.VMEM((7, SIDE, INNER), F32),
            pltpu.VMEM((18, SIDE, INNER), F32),
            pltpu.VMEM((4, SIDE, PADDED, 128), F32),
            pltpu.VMEM((2, 512, 256), BF16),
            pltpu.SemaphoreType.DMA((16,)),
        ],
        compiler_params=pltpu.CompilerParams(vmem_limit_bytes=24 << 20),
        name="ultrasound_last",
    )(*held)


def solution(mesh):
    return jax.shard_map(
        body,
        mesh=mesh,
        in_specs=(
            P(("row", "col"), None, None, None),
            P(("row", "col"), None, None, None),
            P(("row", "col"), None, None),
            P(("row", "col")),
            P(None, "row", "col", None),
            P("row", "col", None),
            P(),
        ),
        out_specs=(
            P(("row", "col"), None, None, None),
            P(("row", "col"), None, None, None),
            P(None, "row", "col", None),
        ),
        check_vma=False,
    )
```

```python
import jax
import jax.numpy as jnp
from jax import lax
from jax.experimental import pallas as pl
from jax.experimental.pallas import tpu as pltpu
from jax.sharding import PartitionSpec as P

STEPS = 3
SIDE = 32
EDGE = 16
PLANES = 36
DEEP = 56
ROWS = 40
PADDED = 40
MAIN_VMEM = 56_000_000
LANES = 640
INNER = 512
MESH = pl.DeviceIdType.MESH
F32 = jnp.float32
BF16 = jnp.bfloat16


def lane_pos(shape):
    return lax.broadcasted_iota(jnp.int32, shape, len(shape) - 1)


def row_pos(shape):
    return lax.broadcasted_iota(jnp.int32, shape, len(shape) - 2)


def shift(value, amount, axis):
    amount = amount % value.shape[axis]
    return value if amount == 0 else pltpu.roll(value, amount, axis)


def across(value, axis, amount):
    return shift(value, -amount, axis) - shift(value, amount, axis)


def pick(indices, table, column):
    bits = [(indices & (1 << bit)) != 0 for bit in range(3)]
    values = [table[level, column] for level in range(8)]
    values = [jnp.where(bits[0], values[2 * i + 1], values[2 * i]) for i in range(4)]
    values = [jnp.where(bits[1], values[2 * i + 1], values[2 * i]) for i in range(2)]
    return jnp.where(bits[2], values[1], values[0])


def rows_of(i):
    return slice(8 * i, 8 * i + 8)


def along_x(ref, f, i, width):
    sub = row_pos((8, width))
    here = ref[f, rows_of(i), 0:width]
    after = ref[f, rows_of((i + 1) % 5), 0:width]
    before = ref[f, rows_of((i + 4) % 5), 0:width]
    forward = shift(jnp.where(sub == 0, after, here), -1, 0)
    backward = shift(jnp.where(sub == 7, before, here), 1, 0)
    return forward - backward


def z_weights(W):
    k = lax.broadcasted_iota(jnp.int32, (128, 128), 0)
    at = lax.broadcasted_iota(jnp.int32, (128, 128), 1)
    depth = at % 16
    up = jnp.logical_and(k == at + 1, depth != 15).astype(F32)
    down = jnp.logical_and(k == at - 1, depth != 0).astype(F32)
    change = (up - down).astype(BF16)
    top = jnp.logical_and(k == at - 15, depth == 15).astype(F32)
    base = jnp.logical_and(k == at + 15, depth == 0).astype(F32)
    for half, sign in ((0, 1.0), (1, -1.0)):
        into_brick, into_water = (-sign * top).astype(BF16), (sign * base).astype(BF16)
        for part in range(2):
            rows = slice(128 * part, 128 * part + 128)
            W[half, rows, 0:128], W[half, rows, 128:256] = change, into_water
            rows = slice(256 + 128 * part, 384 + 128 * part)
            W[half, rows, 0:128], W[half, rows, 128:256] = into_brick, change


def parts(values):
    out = []
    for value in values:
        high = value.astype(BF16)
        out += [high, (value - high.astype(F32)).astype(BF16)]
    return jnp.concatenate(out, axis=1)


def stacked(ref, f, tiles):
    return jnp.concatenate(
        [ref[f, rows_of(i), 128 * t:128 * t + 128] for i, t in tiles], axis=0
    )


def unstacked(value, tiles, i, count):
    none = jnp.zeros((8, 128), F32)
    found = []
    for t in range(count):
        if (i, t) in tiles:
            place = 8 * tiles.index((i, t))
            found.append(value[place:place + 8])
        else:
            found.append(none)
    return jnp.concatenate(found, axis=1)


def times(values, weights):
    return jnp.dot(parts(values), weights, preferred_element_type=F32)


def brick_velocity(group, V, S, G, L, W, V_to, G_to):
    tiles = [(i, t) for i in group for t in range(5) if (i, t) != (4, 4)]
    single = W[0, 0:256, 0:128]
    xz = times([stacked(S, 4, tiles)], single)
    yz = times([stacked(S, 5, tiles)], single)
    both = times([stacked(S, 2, tiles), stacked(S, 6, tiles)], W[0])
    for i in group:
        here = rows_of(i)
        light = L[0, here, :]
        V_to[0, here, :] = V[0, here, :] + light * (
            along_x(S, 0, i, LANES) + across(S[3, here, :], 1, 16)
            + unstacked(xz, tiles, i, 5)
        )
        V_to[1, here, :] = V[1, here, :] + light * (
            along_x(S, 3, i, LANES) + across(S[1, here, :], 1, 16)
            + unstacked(yz, tiles, i, 5)
        )
        V_to[2, here, :] = V[2, here, :] + light * (
            along_x(S, 4, i, LANES) + across(S[5, here, :], 1, 16)
            + unstacked(both[:, 0:128], tiles, i, 5)
        )
        light = L[1, here, :]
        G_to[0, here, :] = G[0, here, :] - light * along_x(S, 6, i, LANES)
        G_to[1, here, :] = G[1, here, :] - light * across(S[6, here, :], 1, 16)
        G_to[2, here, :] = G[2, here, :] - light * unstacked(both[:, 128:256], tiles, i, 5)


def brick_stress(group, V, S, G, CF, M, W, S_to, M_to):
    tiles = [(i, t) for i in group for t in range(4)]
    pair = W[1, :, 0:128]
    z_all = [
        times([stacked(V, 0, tiles), stacked(G, 0, tiles)], pair),
        times([stacked(V, 1, tiles), stacked(G, 1, tiles)], pair),
    ]
    both = times([stacked(V, 2, tiles), stacked(G, 2, tiles)], W[1])
    z_all.append(both[:, 0:128])
    for i in group:
        here = rows_of(i)
        change = along_x(G, 0, i, INNER) + across(G[1, here, :], 1, 16)[:, 0:INNER]
        change = change + unstacked(both[:, 128:256], tiles, i, 4)
        S_to[6, here, 0:INNER] = S[6, here, 0:INNER] - CF[7, here, :] * change
        dx = [along_x(V, k, i, INNER) for k in range(3)]
        dy = [across(V[k, here, :], 1, 16)[:, 0:INNER] for k in range(3)]
        dz = [unstacked(z_all[k], tiles, i, 4) for k in range(3)]
        strain = (
            dx[0], dy[1], dz[2],
            0.5 * (dy[0] + dx[1]), 0.5 * (dz[0] + dx[2]), 0.5 * (dz[1] + dy[2]),
        )
        dilation = dx[0] + dy[1] + dz[2]
        for k in range(6):
            gain = CF[1, here, :] * strain[k]
            relaxed = CF[6, here, :] * strain[k]
            if k < 3:
                gain = gain + CF[0, here, :] * dilation
                relaxed = relaxed + CF[5, here, :] * dilation
            for mechanism in range(3):
                held = M[6 * mechanism + k, here, :]
                held = relaxed + CF[2 + mechanism, here, :] * (held - relaxed)
                M_to[6 * mechanism + k, here, :] = held
                gain = gain - held
            S_to[k, here, 0:INNER] = S[k, here, 0:INNER] + gain


def main_kernel(
    mvs_in, mem_in, mat_in, live_in, water_in, wmat_in, table,
    V, S, G, L, CF, M, PR, U,
    C, ZW, MAT, WS, WM,
    tbx, tby, tbc, twx, twy, sbx, sby, swx, swy,
    rbx, rby, rbc, rwx, rwy, ebx, eby, ewx, ewy,
    load_sem, send_sem, recv_sem, xsend_sem, xrecv_sem,
):
    row, col = lax.axis_index("row"), lax.axis_index("col")
    nrow, ncol = lax.axis_size("row"), lax.axis_size("col")
    row_to = (row < nrow - 1, row > 0)
    row_from = (row > 0, row < nrow - 1)
    col_to = (col < ncol - 1, col > 0)
    col_from = (col > 0, col < ncol - 1)
    step_of = (1, -1)
    inner = pl.ds(8, SIDE)

    def line(field, y):
        return pl.ds(field * PLANES * DEEP + 2 * DEEP + 8 + y, SIDE, stride=DEEP)

    flat_p = PR.reshape(PLANES * DEEP, 128)
    flat_u = U.reshape(3 * PLANES * DEEP, 128)
    flat_c = C.reshape(3 * PLANES * DEEP, 128)
    flat_m = WM.reshape(SIDE * PADDED, 128)

    loads, motion_loads, memory_loads = [], [], []
    for s in range(4):
        rows, lanes = pl.ds(EDGE * (s // 2), EDGE), pl.ds(256 * (s % 2), 256)
        motion_loads += [
            pltpu.make_async_copy(
                mvs_in.at[s, pl.ds(0, 3)], V.at[:, rows, lanes], load_sem.at[s]
            ),
            pltpu.make_async_copy(
                mvs_in.at[s, pl.ds(3, 6)], S.at[pl.ds(0, 6), rows, lanes], load_sem.at[4 + s]
            ),
            pltpu.make_async_copy(mat_in.at[s], MAT.at[rows, lanes], load_sem.at[8 + s]),
        ]
        memory_loads.append(
            pltpu.make_async_copy(mem_in.at[s], M.at[:, rows, lanes], load_sem.at[12 + s])
        )
    pressure_load = pltpu.make_async_copy(
        water_in.at[0], PR.at[pl.ds(2, SIDE), inner], load_sem.at[16]
    )
    velocity_load = pltpu.make_async_copy(
        water_in.at[pl.ds(1, 3)], U.at[:, pl.ds(2, SIDE), inner], load_sem.at[17]
    )
    kind_load = pltpu.make_async_copy(
        wmat_in, WM.at[:, pl.ds(0, SIDE)], load_sem.at[18]
    )
    for load in [pressure_load, velocity_load, kind_load] + motion_loads + memory_loads:
        load.start()

    barrier = pltpu.get_barrier_semaphore()
    partners = []
    for dr in (-1, 0, 1):
        for dc in (-1, 0, 1):
            if dr or dc:
                there = jnp.logical_and(
                    jnp.logical_and(row + dr >= 0, row + dr < nrow),
                    jnp.logical_and(col + dc >= 0, col + dc < ncol),
                )
                partners.append(there)

                @pl.when(there)
                def _():
                    pl.semaphore_signal(
                        barrier, inc=1, device_id=(row + dr, col + dc), device_id_type=MESH
                    )

    for t in range(2):

        @pl.when(jnp.logical_not(row_from[t]))
        def _():
            rbx[:, t] = jnp.zeros((STEPS, EDGE, INNER), F32)
            rwx[:, t] = jnp.zeros((STEPS, 2, SIDE, 128), F32)
            ebx[t] = jnp.zeros((8, INNER), F32)
            ewx[t] = jnp.zeros((2, SIDE, 128), F32)

        @pl.when(jnp.logical_not(col_from[t]))
        def _():
            rby[:, t] = jnp.zeros((STEPS, SIDE, 256), F32)
            rwy[:, t] = jnp.zeros((STEPS, 2, SIDE, 128), F32)
            eby[t] = jnp.zeros((SIDE, 128), F32)
            ewy[t] = jnp.zeros((2, SIDE, 128), F32)

        for u in range(2):

            @pl.when(jnp.logical_not(jnp.logical_and(row_from[t], col_from[u])))
            def _():
                rbc[:, 2 * t + u] = jnp.zeros((STEPS, 8, 128), F32)

    def remote(src, dst, send, recv, dr, dc):
        return pltpu.make_async_remote_copy(
            src_ref=src, dst_ref=dst, send_sem=send, recv_sem=recv,
            device_id=(row + dr, col + dc), device_id_type=MESH,
        )

    def brick_x_copies(n):
        out = []
        for t in range(2):
            d = step_of[t]
            out.append((
                remote(tbx.at[n, t], rbx.at[n, t], send_sem.at[n, t], recv_sem.at[n, t], d, 0),
                row_to[t], row_from[t],
            ))
            for u in range(2):
                q = 2 * t + u
                out.append((
                    remote(tbc.at[n, q], rbc.at[n, q], send_sem.at[n, 4 + q],
                           recv_sem.at[n, 4 + q], d, step_of[u]),
                    jnp.logical_and(row_to[t], col_to[u]),
                    jnp.logical_and(row_from[t], col_from[u]),
                ))
        return out

    def side_copies(x_refs, y_refs, x_sems, y_sems):
        out = []
        for t in range(2):
            d = step_of[t]
            if x_refs:
                out.append((
                    remote(x_refs[0].at[t], x_refs[1].at[t], x_sems[0](t), x_sems[1](t), d, 0),
                    row_to[t], row_from[t],
                ))
            if y_refs:
                out.append((
                    remote(y_refs[0].at[t], y_refs[1].at[t], y_sems[0](t), y_sems[1](t), 0, d),
                    col_to[t], col_from[t],
                ))
        return out

    def step_sems(n, first):
        return (lambda t: send_sem.at[n, first + t]), (lambda t: recv_sem.at[n, first + t])

    def extra_sems(first):
        return (lambda t: xsend_sem.at[first + t]), (lambda t: xrecv_sem.at[first + t])

    def brick_y_copies(n):
        return side_copies(None, (tby.at[n], rby.at[n]), None, step_sems(n, 2))

    def water_x_copies(n):
        return side_copies((twx.at[n], rwx.at[n]), None, step_sems(n, 8), None)

    def water_y_copies(n):
        return side_copies(None, (twy.at[n], rwy.at[n]), None, step_sems(n, 10))

    def first_water_copies():
        return side_copies((swx, ewx), (swy, ewy), extra_sems(0), extra_sems(2))

    def first_brick_copies():
        return side_copies((sbx, ebx), (sby, eby), extra_sems(4), extra_sems(6))

    def start(copies):
        for copy, to, _ in copies:

            @pl.when(to)
            def _():
                copy.start()

    def arrive(copies):
        for copy, _, came in copies:

            @pl.when(came)
            def _():
                copy.wait_recv()

    def sent(copies):
        for copy, to, _ in copies:

            @pl.when(to)
            def _():
                copy.wait_send()

    pair = row_pos((8, INNER))
    tile_lane = lane_pos((SIDE, 128))
    lane, sub = lane_pos((8, 128)), row_pos((8, 128))

    def pack_brick_x(n):
        for half in range(2):
            down, up = jnp.zeros((8, INNER), F32), jnp.zeros((8, INNER), F32)
            for j in range(3 if half else 4):
                k = 4 * half + j
                here = pair // 2 == j
                up = jnp.where(here, shift(S[k, 24:32, 0:INNER], 2 * j - 6, 0), up)
                down = jnp.where(here, shift(S[k, 0:8, 0:INNER], 2 * j, 0), down)
            tbx[n, 0, 8 * half:8 * half + 8, :] = up
            tbx[n, 1, 8 * half:8 * half + 8, :] = down
        for t in range(2):
            rows = slice(24, 32) if t == 0 else slice(0, 8)
            for u in range(2):
                corner = jnp.zeros((8, 128), F32)
                for k in range(6):
                    tile = S[k, rows, 384:512] if u == 0 else S[k, rows, 0:128]
                    tile = shift(tile, 16 * k - (112 if u == 0 else 0), 1)
                    corner = jnp.where(lane // 16 == k, tile, corner)
                tbc[n, 2 * t + u] = corner

    def pack_brick_y(n):
        for half in range(2):
            ahead, back = jnp.zeros((SIDE, 128), F32), jnp.zeros((SIDE, 128), F32)
            for j in range(3 if half else 4):
                k = 4 * half + j
                here = tile_lane // 32 == j
                ahead = jnp.where(here, shift(S[k, 0:SIDE, 384:512], 32 * j - 96, 1), ahead)
                back = jnp.where(here, shift(S[k, 0:SIDE, 0:128], 32 * j, 1), back)
            tby[n, 0, :, 128 * half:128 * half + 128] = ahead
            tby[n, 1, :, 128 * half:128 * half + 128] = back

    def unpack_brick_x(n):
        for k in range(7):
            tile, j = k // 4, k % 4
            rows = rows_of(tile)
            before = shift(rbx[n, 0, rows, :], 6 - 2 * j, 0)
            after = shift(rbx[n, 1, rows, :], -2 * j, 0)
            S[k, 32:40, 0:INNER] = jnp.where(pair < 4, after, before)
        for k in range(6):
            top = jnp.where(
                lane < 64, shift(rbc[n, 3], -16 * k, 1), shift(rbc[n, 2], 112 - 16 * k, 1)
            )
            bottom = jnp.where(
                lane < 64, shift(rbc[n, 1], -16 * k, 1), shift(rbc[n, 0], 112 - 16 * k, 1)
            )
            S[k, 32:40, INNER:LANES] = jnp.where(sub < 4, top, bottom)

    def unpack_brick_y(n):
        for k in range(7):
            tile, j = k // 4, k % 4
            lanes = slice(128 * tile, 128 * tile + 128)
            before = shift(rby[n, 0, :, lanes], 96 - 32 * j, 1)
            after = shift(rby[n, 1, :, lanes], -32 * j, 1)
            S[k, 0:SIDE, INNER:LANES] = jnp.where(tile_lane < 64, after, before)

    x_extra = ((V, 0), (V, 1), (V, 2), (L, 0), (G, 0), (L, 1))
    y_extra = ((V, 0), (V, 1), (V, 2), (L, 0), (G, 1), (L, 1))

    def pack_first_brick():
        down, up = jnp.zeros((8, INNER), F32), jnp.zeros((8, INNER), F32)
        ahead, back = jnp.zeros((SIDE, 128), F32), jnp.zeros((SIDE, 128), F32)
        for j in range(6):
            ref, f = x_extra[j]
            up = jnp.where(pair == j, shift(ref[f, 24:32, 0:INNER], j - 7, 0), up)
            down = jnp.where(pair == j, shift(ref[f, 0:8, 0:INNER], j, 0), down)
            ref, f = y_extra[j]
            here = tile_lane // 16 == j
            ahead = jnp.where(here, shift(ref[f, 0:SIDE, 384:512], 16 * j - 112, 1), ahead)
            back = jnp.where(here, shift(ref[f, 0:SIDE, 0:128], 16 * j, 1), back)
        sbx[0], sbx[1], sby[0], sby[1] = up, down, ahead, back

    def unpack_first_brick():
        for j in range(6):
            ref, f = x_extra[j]
            ref[f, 32:40, 0:INNER] = jnp.where(
                pair < 4, shift(ebx[1], -j, 0), shift(ebx[0], 7 - j, 0)
            )
            ref, f = y_extra[j]
            ref[f, 0:SIDE, INNER:LANES] = jnp.where(
                tile_lane < 64, shift(eby[1], -16 * j, 1), shift(eby[0], 112 - 16 * j, 1)
            )

    def pack_water_x(n):
        for k in range(2):
            twx[n, 0, k] = PR[32 + k, inner, :]
            twx[n, 1, k] = PR[2 + k, inner, :]

    def pack_water_y(n):
        for k in range(2):
            twy[n, 0, k] = flat_p[line(0, 30 + k), :]
            twy[n, 1, k] = flat_p[line(0, k), :]

    def unpack_water(n):
        for k in range(2):
            PR[k, inner, :] = rwx[n, 0, k]
            PR[34 + k, inner, :] = rwx[n, 1, k]
            flat_p[line(0, k - 2), :] = rwy[n, 0, k]
            flat_p[line(0, 32 + k), :] = rwy[n, 1, k]

    def pack_first_water():
        for t in range(2):
            end = SIDE - 1 if t == 0 else 0
            swx[t, 0] = U[0, 2 + end, inner, :]
            swx[t, 1] = 0.5 * pick(WM[end, 0:SIDE, :], table, 0)
            swy[t, 0] = flat_u[line(1, end), :]
            swy[t, 1] = 0.5 * pick(flat_m[pl.ds(end, SIDE, stride=PADDED), :], table, 0)

    def unpack_first_water():
        U[0, 1, inner, :], C[0, 1, inner, :] = ewx[0, 0], ewx[0, 1]
        U[0, 34, inner, :], C[0, 34, inner, :] = ewx[1, 0], ewx[1, 1]
        flat_u[line(1, -1), :], flat_c[line(0, -1), :] = ewy[0, 0], ewy[0, 1]
        flat_u[line(1, 32), :], flat_c[line(0, 32), :] = ewy[1, 0], ewy[1, 1]

    def to_slab(ref, f, rows_at):
        for t in range(4):
            value = rows_at(8 * t)
            for j in range(1, 8):
                moved = shift(rows_at(8 * t + j), 16 * j, 1)
                value = jnp.where(tile_lane // 16 == j, moved, value)
            if f is None:
                ref[:, 128 * t:128 * t + 128] = value
            else:
                ref[f, 0:SIDE, 128 * t:128 * t + 128] = value

    plane_lane = lane_pos((SIDE, 128))
    wide, above_rows, below_rows = pl.ds(7, 40), pl.ds(8, 40), pl.ds(6, 40)

    def x_velocity(x_at):
        U[0, x_at, inner] -= C[0, x_at, inner] * (PR[x_at + 1, inner] - PR[x_at - 1, inner])

    def water_velocity(x_at):
        x_velocity(x_at)
        U[1, x_at, wide] -= C[0, x_at, wide] * (PR[x_at, above_rows] - PR[x_at, below_rows])
        p = PR[x_at, inner]
        U[2, x_at, inner] -= C[2, x_at, inner] * (
            jnp.where(plane_lane == 0, 0.0, p) - shift(p, 2, 1)
        )

    def water_pressure(x_at):
        change = U[0, x_at + 1, inner] - U[0, x_at - 1, inner]
        change = change + (U[1, x_at, pl.ds(9, SIDE)] - U[1, x_at, pl.ds(7, SIDE)])
        w = U[2, x_at, inner]
        change = change + (jnp.where(plane_lane == 127, 0.0, shift(w, -2, 1)) - w)
        PR[x_at, inner] -= C[1, x_at, inner] * change

    def water_ends():
        x_velocity(1)
        x_velocity(34)
        for x_at in (2, 3, 4, 5, 30, 31, 32, 33):
            water_velocity(x_at)
        for x_at in (2, 3, 32, 33):
            water_pressure(x_at)

    def water_rest():
        def velocity(x, carry):
            for plane in range(4):
                water_velocity(4 * x + (6 + plane))
            return carry

        lax.fori_loop(0, 6, velocity, 0)

        def pressure(x, carry):
            for plane in range(4):
                water_pressure(4 * x + (4 + plane))
            return carry

        lax.fori_loop(0, 7, pressure, 0)

    pressure_load.wait()
    velocity_load.wait()
    kind_load.wait()
    pack_water_x(0)
    pack_water_y(0)
    pack_first_water()
    for load in motion_loads:
        load.wait()
    live = [live_in[s].astype(F32) for s in range(4)]

    def alive_of(i):
        left = lane_pos((8, INNER)) < 256
        return jnp.where(
            left, jnp.where(i < 2, live[0], live[2]), jnp.where(i < 2, live[1], live[3])
        )

    def strip(i):
        return pl.ds(pl.multiple_of(8 * i, 8), 8)

    def motion_start(i, carry):
        here = strip(i)
        alive = alive_of(i)
        for k in range(3):
            V[k, here, 0:INNER] = V[k, here, 0:INNER] * alive
        for k in range(6):
            S[k, here, 0:INNER] = S[k, here, 0:INNER] * alive
        L[0, here, 0:INNER] = 0.5 * alive * pick(MAT[here, :], table, 0)
        return carry

    lax.fori_loop(0, 4, motion_start, 0)
    to_slab(S, 6, lambda y: flat_p[line(0, y), :])
    pack_brick_x(0)
    pack_brick_y(0)
    count = partners[0].astype(jnp.int32)
    for there in partners[1:]:
        count = count + there.astype(jnp.int32)
    pl.semaphore_wait(barrier, count)
    start(water_x_copies(0))
    start(water_y_copies(0))
    start(first_water_copies())
    start(brick_x_copies(0))
    start(brick_y_copies(0))
    to_slab(G, 0, lambda y: flat_u[line(0, y), :])
    to_slab(G, 1, lambda y: flat_u[line(1, y), :])
    to_slab(WS, None, lambda y: flat_m[pl.ds(y, SIDE, stride=PADDED), :])

    def slab_params(i, carry):
        here = strip(i)
        L[1, here, 0:INNER] = 0.5 * pick(WS[here, :], table, 0)
        CF[7, here, :] = 0.5 * pick(WS[here, :], table, 1)
        return carry

    lax.fori_loop(0, 4, slab_params, 0)
    pack_first_brick()
    start(first_brick_copies())
    to_slab(G, 2, lambda y: flat_u[line(2, y), :])
    z_weights(ZW)

    def water_params(x, carry):
        for plane in range(2):
            kinds = WM[2 * x + plane, 0:SIDE]
            x_at = 2 * x + (2 + plane)
            light = 0.5 * pick(kinds, table, 0)
            C[0, x_at, inner] = light
            C[1, x_at, inner] = 0.5 * pick(kinds, table, 1)
            C[2, x_at, inner] = shift(light, 1, 1)
            U[2, x_at, inner] = shift(U[2, x_at, inner], 1, 1)
        return carry

    lax.fori_loop(0, SIDE // 2, water_params, 0)
    for load in memory_loads:
        load.wait()

    def memory_start(i, carry):
        here = strip(i)
        alive = alive_of(i)
        kinds = MAT[here, :]
        CF[0, here, :] = 0.5 * alive * pick(kinds, table, 1)
        CF[1, here, :] = alive * pick(kinds, table, 2)
        for mechanism in range(3):
            CF[2 + mechanism, here, :] = pick(kinds, table, 3 + mechanism)
        CF[5, here, :] = 0.5 * alive * pick(kinds, table, 6)
        CF[6, here, :] = alive * pick(kinds, table, 7)
        for k in range(18):
            M[k, here, :] = M[k, here, :] * alive
        return carry

    lax.fori_loop(0, 4, memory_start, 0)
    arrive(first_water_copies())
    unpack_first_water()

    def step(n, carry):
        arrive(water_y_copies(n))
        arrive(water_x_copies(n))
        unpack_water(n)
        water_ends()
        pack_water_x(n + 1)
        start(water_x_copies(n + 1))
        water_rest()
        pack_water_y(n + 1)
        start(water_y_copies(n + 1))

        @pl.when(n == 0)
        def _():
            arrive(first_brick_copies())
            unpack_first_brick()

        arrive(brick_y_copies(n))
        unpack_brick_y(n)
        brick_velocity((1, 2), V, S, G, L, ZW, V, G)
        arrive(brick_x_copies(n))
        unpack_brick_x(n)
        brick_velocity((0, 3, 4), V, S, G, L, ZW, V, G)
        brick_stress((0, 3), V, S, G, CF, M, ZW, S, M)
        pack_brick_x(n + 1)
        start(brick_x_copies(n + 1))
        brick_stress((1, 2), V, S, G, CF, M, ZW, S, M)
        pack_brick_y(n + 1)
        start(brick_y_copies(n + 1))
        return carry

    lax.fori_loop(0, STEPS - 1, step, 0)
    last = STEPS - 1
    arrive(water_y_copies(last))
    arrive(water_x_copies(last))
    unpack_water(last)
    water_ends()
    water_rest()

    def settle(x, carry):
        for plane in range(4):
            x_at = 4 * x + (2 + plane)
            U[2, x_at, inner] = shift(U[2, x_at, inner], -1, 1)
        return carry

    lax.fori_loop(0, SIDE // 4, settle, 0)
    sent(first_water_copies())
    sent(first_brick_copies())
    for n in range(STEPS):
        sent(water_x_copies(n))
        sent(water_y_copies(n))
        sent(brick_x_copies(n))
        sent(brick_y_copies(n))
    arrive(brick_y_copies(last))
    unpack_brick_y(last)
    arrive(brick_x_copies(last))
    unpack_brick_x(last)


def last_kernel(
    V, S, G, L, CF, M, PR, U,
    motion_out, memory_out, water_out,
    V_to, G_to, S_to, M_to, W_to, ZW, sem,
):
    z_weights(ZW)
    for group in ((0, 1), (2, 3), (4,)):
        brick_velocity(group, V, S, G, L, ZW, V_to, G_to)
    stores = []

    def store(half):
        for s in (2 * half, 2 * half + 1):
            rows, lanes = pl.ds(EDGE * half, EDGE), pl.ds(256 * (s % 2), 256)
            for copy in (
                pltpu.make_async_copy(
                    V_to.at[:, rows, lanes], motion_out.at[s, pl.ds(0, 3)], sem.at[s]
                ),
                pltpu.make_async_copy(
                    S_to.at[pl.ds(0, 6), rows, lanes], motion_out.at[s, pl.ds(3, 6)],
                    sem.at[4 + s],
                ),
                pltpu.make_async_copy(
                    M_to.at[:, rows, lanes], memory_out.at[s], sem.at[8 + s]
                ),
            ):
                copy.start()
                stores.append(copy)

    for half in range(2):
        brick_stress(
            (2 * half, 2 * half + 1), V_to, S, G_to, CF, M, ZW, S_to, M_to
        )
        store(half)
    tile_lane = lane_pos((SIDE, 128))
    flat_p = PR.reshape(PLANES * DEEP, 128)
    flat_u = U.reshape(3 * PLANES * DEEP, 128)
    flat_to = W_to.reshape(4 * SIDE * PADDED, 128)
    for field in range(4):
        ref, f = ((S_to, 6), (G_to, 0), (G_to, 1), (G_to, 2))[field]
        main = flat_p if field == 0 else flat_u
        base = 2 * DEEP + 8 + max(field - 1, 0) * PLANES * DEEP
        for t in range(4):
            value = ref[f, 0:SIDE, 128 * t:128 * t + 128]
            for j in range(8):
                y = 8 * t + j
                flat_to[pl.ds(field * SIDE * PADDED + y, SIDE, stride=PADDED), :] = jnp.where(
                    tile_lane < 8,
                    shift(value, -16 * j, 1),
                    main[pl.ds(base + y, SIDE, stride=DEEP), :],
                )
        stores.append(
            pltpu.make_async_copy(
                W_to.at[field, :, pl.ds(0, SIDE)], water_out.at[field], sem.at[12 + field]
            )
        )
        stores[-1].start()
    for copy in stores:
        copy.wait()


def body(*args):
    any_space = pl.BlockSpec(memory_space=pltpu.HBM)
    smem = pl.BlockSpec(memory_space=pltpu.SMEM)
    vmem = pl.BlockSpec(memory_space=pltpu.VMEM)
    messages = [
        (STEPS, 2, EDGE, INNER), (STEPS, 2, SIDE, 256), (STEPS, 4, 8, 128),
        (STEPS, 2, 2, SIDE, 128), (STEPS, 2, 2, SIDE, 128),
        (2, 8, INNER), (2, SIDE, 128), (2, 2, SIDE, 128), (2, 2, SIDE, 128),
    ]
    messages = [pltpu.VMEM(shape, F32) for shape in messages]
    state = [
        (3, ROWS, LANES), (7, ROWS, LANES), (3, ROWS, LANES), (2, ROWS, LANES),
        (8, SIDE, INNER), (18, SIDE, INNER),
        (PLANES, DEEP, 128), (3, PLANES, DEEP, 128),
    ]
    held = pl.pallas_call(
        main_kernel,
        out_shape=tuple(pltpu.VMEM(shape, F32) for shape in state),
        in_specs=[any_space, any_space, any_space, smem, any_space, any_space, smem],
        out_specs=(vmem,) * len(state),
        scratch_shapes=[
            pltpu.VMEM((3, PLANES, DEEP, 128), F32),
            pltpu.VMEM((2, 512, 256), BF16),
            pltpu.VMEM((SIDE, INNER), jnp.int32),
            pltpu.VMEM((SIDE, INNER), jnp.int32),
            pltpu.VMEM((SIDE, PADDED, 128), jnp.int32),
            *messages,
            *messages,
            pltpu.SemaphoreType.DMA((19,)),
            pltpu.SemaphoreType.DMA((STEPS, 12)),
            pltpu.SemaphoreType.DMA((STEPS, 12)),
            pltpu.SemaphoreType.DMA((8,)),
            pltpu.SemaphoreType.DMA((8,)),
        ],
        compiler_params=pltpu.CompilerParams(
            collective_id=0, has_side_effects=True, vmem_limit_bytes=MAIN_VMEM
        ),
        name="ultrasound_steps",
    )(*args)
    return pl.pallas_call(
        last_kernel,
        out_shape=(
            jax.ShapeDtypeStruct((4, 9, EDGE, 256), F32),
            jax.ShapeDtypeStruct((4, 18, EDGE, 256), F32),
            jax.ShapeDtypeStruct((4, SIDE, SIDE, 128), F32),
        ),
        in_specs=[vmem] * 8,
        out_specs=(any_space,) * 3,
        scratch_shapes=[
            pltpu.VMEM((3, ROWS, LANES), F32),
            pltpu.VMEM((3, ROWS, LANES), F32),
            pltpu.VMEM((7, SIDE, INNER), F32),
            pltpu.VMEM((18, SIDE, INNER), F32),
            pltpu.VMEM((4, SIDE, PADDED, 128), F32),
            pltpu.VMEM((2, 512, 256), BF16),
            pltpu.SemaphoreType.DMA((16,)),
        ],
        compiler_params=pltpu.CompilerParams(vmem_limit_bytes=24 << 20),
        name="ultrasound_last",
    )(*held)


def solution(mesh):
    return jax.shard_map(
        body,
        mesh=mesh,
        in_specs=(
            P(("row", "col"), None, None, None),
            P(("row", "col"), None, None, None),
            P(("row", "col"), None, None),
            P(("row", "col")),
            P(None, "row", "col", None),
            P("row", "col", None),
            P(),
        ),
        out_specs=(
            P(("row", "col"), None, None, None),
            P(("row", "col"), None, None, None),
            P(None, "row", "col", None),
        ),
        check_vma=False,
    )
```
